32 devices in a mesh: section: 2 (over core), ctx: 16 (over z, y, x).
Axes of the slice: x: 2, y: 2, z: 4, core: 2. Of those that a mesh axis runs over, the one named last changes fastest.
Arguments:
- tokens: bfloat16 [2, 2048, 2048], P(None, 'ctx'), may hold values from -6 to 6
- qkv_weight: bfloat16 [2, 2048, 3072], P('section', 'ctx'), may hold values from -0.125 to 0.125
- out_weight: bfloat16 [2, 1024, 2048], P('section', 'ctx'), may hold values from -0.1875 to 0.1875
- log_decay: float32 [2, 2, 2048, 16], P('section', None, 'ctx'), may hold values from -1.5 to 0, as said below
Outputs:
- hidden_states: bfloat16 [2, 2, 2048, 2048], P('section', None, 'ctx')
The draws below stay inside these ranges and needn't reach their ends.
Inputs may be any that keep to these rules, and one draw needn't show every extreme that they name: `log_decay`: every value is negative.
All inputs are finite; a program needn't handle non-finite values.
Results may differ from the reference program's by a relative error of at most 0.025.
Values may be sent and summed in bfloat16 or wider, within the bound.
A program may use at most 128 MiB of HBM per device.

```python
import jax
import jax.numpy as jnp
from jax import lax

D = 2048
MIXER_HEADS = 16
HEAD = 64
TOK_DEV = 128
MICRO_BATCHES = 2
LAYER_TOTAL = 2
SEQUENCE_LENGTH = 2048
N_CTX = 16


def draw_log_decay(key, part):
    key_rows_list = jax.random.split(key, 7)
    slow_share = 0.5
    head_shape = (LAYER_TOTAL, 1, 1, 1, MIXER_HEADS)
    slow_heads = jax.random.bernoulli(key_rows_list[0], slow_share, head_shape)
    fast_rate = jax.random.uniform(key_rows_list[1], head_shape, jnp.float32, 1.0 / 50.0, 1.0 / 30.0)
    slow_total = jax.random.uniform(key_rows_list[2], head_shape, jnp.float32, 0.1, 0.45)
    base_rate = jnp.where(slow_heads, slow_total / SEQUENCE_LENGTH, fast_rate)
    device_factor = jax.random.uniform(key_rows_list[3], (LAYER_TOTAL, MICRO_BATCHES, N_CTX, 1, MIXER_HEADS), jnp.float32, 0.6, 1.4)
    position_factor = jnp.clip(1.0 + 0.2 * jax.random.normal(key_rows_list[4], (LAYER_TOTAL, MICRO_BATCHES, N_CTX, TOK_DEV, MIXER_HEADS), jnp.float32), 0.6, 1.4)
    decay_rate = (base_rate * device_factor * position_factor).reshape(LAYER_TOTAL, MICRO_BATCHES, SEQUENCE_LENGTH, MIXER_HEADS)
    spurt_position_list = jax.random.randint(key_rows_list[5], (LAYER_TOTAL, MICRO_BATCHES, 2), 0, SEQUENCE_LENGTH)
    spurt_keep_mask = jax.random.uniform(key_rows_list[6], (LAYER_TOTAL, MICRO_BATCHES, 2, MIXER_HEADS), jnp.float32, 0.5, 0.8)
    position_index = jnp.arange(SEQUENCE_LENGTH, dtype=jnp.int32)
    match_count = (position_index[None, None, None, :] == spurt_position_list[:, :, :, None]).astype(jnp.float32)
    spurt_state_sum = jnp.einsum('kgay,kgae->kgye', match_count, jnp.log(spurt_keep_mask))
    return -decay_rate + spurt_state_sum


def block_levels(own_key, shape, cuts, least, largest):
    def one(dim, blocks):
        heights = jax.random.uniform(jax.random.fold_in(jax.random.fold_in(own_key, 6), dim), (blocks,), jnp.float32, least / len(cuts), largest / len(cuts))
        return jnp.repeat(jnp.exp(heights), shape[dim] // blocks).reshape((-1,) + (1,) * (len(shape) - dim - 1))

    gain = one(*cuts[0])
    for cut in cuts[1:]:
        gain = gain * one(*cut)
    return gain


def noise(rng, shape, spread, reach, pieces=(), kind=jnp.bfloat16):
    gain = block_levels(rng, shape, pieces, -0.22, 0.18) if pieces else 1.0
    entries = jax.random.normal(rng, shape, jnp.float32) * spread * gain
    return jnp.minimum(jnp.maximum(entries, -reach), reach).astype(kind)


def setup_inputs(seed: int = 0) -> dict:
    key_of = jax.random.split(jax.random.key(seed), 5)
    tokens = noise(key_of[0], (MICRO_BATCHES, SEQUENCE_LENGTH, D), 1.0, 6.0, ((1, 16),))
    qkv_weight = noise(key_of[1], (LAYER_TOTAL, D, 3 * MIXER_HEADS * HEAD), D ** -0.5, 0.125, ((0, 2), (1, 16)))
    out_weight = noise(key_of[2], (LAYER_TOTAL, MIXER_HEADS * HEAD, D), (MIXER_HEADS * HEAD) ** -0.5, 0.1875, ((0, 2), (1, 16)))
    log_decay = draw_log_decay(jax.random.fold_in(key_of[4], 71), 0)
    return {"tokens": tokens, "qkv_weight": qkv_weight, "out_weight": out_weight, "log_decay": log_decay}


def round_low(value_rows):
    return lax.optimization_barrier(value_rows.astype(jnp.bfloat16)).astype(jnp.float32)

def apply_layer(inputs, weight, out_proj, decay):
    seq_len, model_width = inputs.shape
    head_count = decay.shape[1]
    wide_input = inputs.astype(jnp.float32)
    normed = (wide_input * lax.rsqrt(lax.optimization_barrier(jnp.mean(wide_input * wide_input, axis=-1, keepdims=True)) + 1e-05)).astype(jnp.bfloat16)
    projected = jnp.dot(normed, weight, preferred_element_type=jnp.float32).astype(jnp.bfloat16)
    inner = projected.shape[1] // 3
    head_dim = inner // head_count
    blocks = seq_len // TOK_DEV
    query_rows = projected[:, :inner].reshape(blocks, TOK_DEV, head_count, head_dim).astype(jnp.float32)
    key_block = projected[:, inner:2 * inner].reshape(blocks, TOK_DEV, head_count, head_dim).astype(jnp.float32)
    value_rows = projected[:, 2 * inner:].reshape(blocks, TOK_DEV, head_count, head_dim).astype(jnp.float32)
    cumulative = jnp.cumsum(decay.reshape(blocks, TOK_DEV, head_count), axis=1)
    ending = cumulative[:, -1]
    key_rows_scaled = round_low(key_block * jnp.exp(ending[:, None, :] - cumulative)[..., None])
    block_state = jnp.einsum('bjhk,bjhv->bhkv', key_rows_scaled, value_rows)
    totals = jnp.exp(ending)

    def carry_step(carried, block_item):
        block_total, state_here = block_item
        return (block_total[:, None, None] * carried + state_here, carried)
    start = jnp.zeros((head_count, head_dim, head_dim), jnp.float32)
    _, carried = lax.scan(carry_step, start, (totals, block_state))
    carried_state_low = round_low(carried)
    scores = jnp.einsum('bthk,bjhk->bhtj', query_rows, key_block)
    per_head = jnp.transpose(cumulative, (0, 2, 1))
    decay_gap = per_head[:, :, :, None] - per_head[:, :, None, :]
    position_index = jnp.arange(TOK_DEV, dtype=jnp.int32)
    causal = position_index[:, None] >= position_index[None, :]
    weights = round_low(jnp.where(causal, scores * jnp.exp(jnp.where(causal, decay_gap, 0.0)), 0.0))
    intra_out = jnp.einsum('bhtj,bjhv->bthv', weights, value_rows)
    inter_out = jnp.einsum('bthk,bhkv->bthv', query_rows, carried_state_low) * jnp.exp(cumulative)[..., None]
    mixture = intra_out + inter_out
    normed_out = mixture * lax.rsqrt(lax.optimization_barrier(jnp.mean(mixture * mixture, axis=-1, keepdims=True)) + 1e-05)
    mixed_low = normed_out.reshape(seq_len, inner).astype(jnp.bfloat16)
    mixed = jnp.dot(mixed_low, out_proj, preferred_element_type=jnp.float32)
    return (wide_input + mixed).astype(jnp.bfloat16)

def reference(tokens, qkv_weight, out_weight, log_decay):
    layer_outputs = []
    current = [tokens[micro_index] for micro_index in range(MICRO_BATCHES)]
    for layer_index in range(LAYER_TOTAL):
        current = [apply_layer(current[micro_index], qkv_weight[layer_index], out_weight[layer_index], log_decay[layer_index, micro_index]) for micro_index in range(MICRO_BATCHES)]
        layer_outputs.append(jnp.stack(current, axis=0))
    return jnp.stack(layer_outputs, axis=0)
```

```python
import functools

import jax
import jax.numpy as jnp
import numpy as np
from jax import lax
from jax.experimental import pallas as pl
from jax.experimental.pallas import tpu as pltpu
from jax.sharding import PartitionSpec as P

MESH = pl.DeviceIdType.MESH
TILE = 16


def line_sizes(mesh):
    total = mesh.shape["ctx"]
    places = np.moveaxis(mesh.devices, mesh.axis_names.index("ctx"), 0).reshape(total, -1)[:, 0]
    sizes, left = [], total
    try:
        coords = [tuple(d.coords) for d in places]
    except AttributeError:
        coords = None
    if coords is not None:
        step = 1
        while step < total:
            changed = [a != b for a, b in zip(coords[0], coords[step])]
            axis = changed.index(True)
            size = 1
            while step * size < total and (
                size == 1 or (coords[step * size][axis] != coords[0][axis]
                and all(coords[step * size][i] == coords[0][i] for i in range(3) if i != axis))
            ):
                size += 1
            while total % (step * size):
                size -= 1
            sizes.insert(0, size)
            step *= size
    else:
        while left > 1:
            sizes.append(2)
            left //= 2
    return tuple(sizes)


def pair_axis(sizes):
    return next(i for i, s in enumerate(sizes) if s % 2 == 0)


def pieces(rows, sizes):
    d, axis = len(sizes), pair_axis(sizes)
    rest = tuple(i for i in range(d) if i != axis)
    turned = rest[::-1]
    first, second = (axis,) + turned, (axis,) + rest
    units = rows // TILE
    if units < 2:
        return [(first, first, 0, rows)]
    if units < 8:
        half = units // 2 * TILE
        return [(first, first, 0, half), (second, second, half, rows - half)]
    orders = [
        (first, first, 3), (second, second, 3),
        (turned + (axis,), first, 1), (rest + (axis,), second, 1),
    ]
    shares = [s * units // 8 for _, _, s in orders]
    shares[0] += units - sum(shares)
    out, at = [], 0
    for (near, far, _), share in zip(orders, shares):
        out.append((near, far, at * TILE, share * TILE))
        at += share
    return out


def dot(a, b, contract=((1,), (0,)), precision=None):
    return lax.dot_general(
        a, b, (contract, ((), ())), precision=precision, preferred_element_type=jnp.float32
    )


def whole_kernel(
    sizes, sections, plan, heads, tokens, decay, shard_a, shard_b, out,
    full_a, full_b, xbuf, scales, proj, decays, cumx, cumt, intra, mixed, mixed_in, result,
    items, got, carried, landed,
    send_sem, recv_sem, own_sem, x_send, x_recv, d_sem, mix_sem, start_sem, s1, r1, s2, r2,
):
    f32, bf16 = jnp.float32, jnp.bfloat16
    both = jnp.logical_and
    d = len(sizes)
    axis = pair_axis(sizes)
    total = int(np.prod(sizes))
    strides = [int(np.prod(sizes[i + 1 :])) for i in range(d)]
    me = lax.axis_index("ctx")
    section = lax.axis_index("section")

    def coords_of(index):
        return [lax.rem(lax.div(index, strides[i]), sizes[i]) for i in range(d)]

    mine = coords_of(me)
    role = lax.rem(mine[axis], 2)
    partner = me + (1 - 2 * role) * strides[axis]
    peers = total // 2
    wide = strides[axis] * sizes[axis]

    def peer_of(index):
        line = lax.rem(lax.div(index, strides[axis]), sizes[axis])
        return (
            lax.div(index, wide) * (wide // 2)
            + lax.div(line, 2) * strides[axis]
            + lax.rem(index, strides[axis])
        )

    def device_of(peer, side):
        line = lax.rem(lax.div(peer, strides[axis]), sizes[axis] // 2)
        return (
            lax.div(peer, wide // 2) * wide
            + (2 * line + side) * strides[axis]
            + lax.rem(peer, strides[axis])
        )

    my_peer = peer_of(me)

    slots, ways = 0, []
    for i in range(d):
        for sign in (1, -1):
            ways.append((i, sign, slots if sizes[i] == 2 or sign == 1 else slots + 1))
        slots += 1 if sizes[i] == 2 else 2
    _, micro, rows, width = xbuf.shape
    half_inner = mixed.shape[2]
    half_heads = heads // 2
    head_dim = half_inner // half_heads
    pairs = half_heads // 2
    lanes = 2 * head_dim
    part = carried.shape[2]
    depth_a, depth_b = shard_a.shape[0], shard_b.shape[0]

    staged_a = []
    for h in range(2):
        for which in range(3):
            staged_a.append(
                pltpu.make_async_copy(
                    shard_a.at[:, pl.ds((2 * which + h) * half_inner, half_inner)],
                    full_a.at[
                        h, pl.ds(pl.multiple_of(me * depth_a, TILE), depth_a),
                        pl.ds(which * half_inner, half_inner),
                    ],
                    own_sem.at[2 + 3 * h + which],
                )
            )
    staged_b = pltpu.make_async_copy(
        shard_b, full_b.at[pl.ds(pl.multiple_of(me * depth_b, TILE), depth_b)], own_sem.at[0]
    )
    x_own = pltpu.make_async_copy(tokens, xbuf.at[role], own_sem.at[1])
    for c in staged_a:
        c.start()
    staged_b.start()

    @pl.when(section == 0)
    def _():
        x_own.start()

    barrier = pltpu.get_barrier_semaphore()

    @pl.loop(1, total)
    def _(k):
        pl.semaphore_signal(
            barrier, inc=1, device_id={"ctx": lax.rem(me + k, total)}, device_id_type=MESH
        )

    for away in (-1, 1):
        near = section + away

        @pl.when(both(near >= 0, near < sections))
        def _(near=near):
            for chip in (me, partner):
                pl.semaphore_signal(
                    barrier, inc=1, device_id={"section": near, "ctx": chip}, device_id_type=MESH
                )

    greeted = (section > 0).astype(jnp.int32) + (section < sections - 1).astype(jnp.int32)
    pl.semaphore_wait(barrier, 2 * greeted + (total - 1))

    parts = [(0, h) + p for h in range(2) for p in plan[0]] + [(1, None) + p for p in plan[1]]

    def copy(source, index, way):
        a, h, _, _, at, size = parts[index]
        i, sign, slot = way
        depth = (depth_a, depth_b)[a]
        span = pl.ds(pl.multiple_of(source * depth + at, TILE), size)
        target = full_a.at[h, span] if a == 0 else full_b.at[span]
        return pltpu.make_async_remote_copy(
            src_ref=target,
            dst_ref=target,
            send_sem=send_sem.at[source, index, slot],
            recv_sem=recv_sem.at[source, index],
            device_id={"ctx": me + sign * strides[i]},
            device_id_type=MESH,
        )

    def inside(i, place):
        return both(place >= 0, place < sizes[i])

    def onward(source, coords, index, act):
        _, h, near, far, _, _ = parts[index]
        wanted_here = None if h is None else role == h
        matches = None if near == far or h is None else lax.rem(coords[axis], 2) == h

        def goes(order, i):
            ok = None
            for later in order[order.index(i) + 1 :]:
                same = mine[later] == coords[later]
                ok = same if ok is None else both(ok, same)
            if h is not None and i != axis and order.index(axis) < order.index(i):
                ok = wanted_here if ok is None else both(ok, wanted_here)
            return jnp.bool_(True) if ok is None else ok

        for way in ways:
            i, sign, _ = way
            ok = both(inside(i, mine[i] + sign), (mine[i] - coords[i]) * sign >= 0)
            if h is not None and i == axis:
                ok = both(
                    ok, jnp.logical_or(role != h, inside(i, mine[i] + 2 * sign))
                )
            if matches is None:
                ok = both(ok, goes(near, i))
            else:
                ok = both(
                    ok,
                    jnp.logical_or(
                        both(matches, goes(near, i)), both(jnp.logical_not(matches), goes(far, i))
                    ),
                )

            @pl.when(ok)
            def _(way=way):
                act(copy(source, index, way))

    def arrives(coords, index):
        _, h, near, far, _, _ = parts[index]
        if h is None:
            return None
        gap = mine[axis] - coords[axis]
        beyond = jnp.where(gap > 0, inside(axis, mine[axis] + 1), inside(axis, mine[axis] - 1))
        reach = jnp.logical_or(jnp.logical_or(gap == 0, role == h), beyond)
        in_line = None
        for i in range(d):
            if i != axis:
                same = mine[i] == coords[i]
                in_line = same if in_line is None else both(in_line, same)
        if in_line is None:
            return reach
        by_axis = jnp.logical_or(role == h, both(in_line, reach))

        def by(order):
            return by_axis if order[0] == axis else reach

        if near == far:
            return by(near)
        matches = lax.rem(coords[axis], 2) == h
        return jnp.logical_or(both(matches, by(near)), both(jnp.logical_not(matches), by(far)))

    def of(wanted):
        return [index for index in range(len(parts)) if parts[index][0] == wanted]

    def receive(wanted, least, most):
        @pl.loop(least * total, most * total)
        def _(k):
            hops, j = lax.div(k, total), lax.rem(k, total)
            source = lax.rem(me + j, total)
            coords = coords_of(source)
            away = sum(jnp.abs(mine[i] - coords[i]) for i in range(d))

            @pl.when(away == hops)
            def _():
                for index in of(wanted):
                    def take(index=index):
                        copy(source, index, ways[0]).wait_recv()
                        onward(source, coords, index, lambda c: c.start())

                    ok = arrives(coords, index)
                    if ok is None:
                        take()
                    else:
                        pl.when(ok)(take)

    def drain(wanted):
        @pl.loop(0, total)
        def _(source):
            coords = coords_of(source)
            for index in of(wanted):
                got_it = arrives(coords, index)

                def wait(index=index):
                    onward(source, coords, index, lambda c: c.wait_send())

                if got_it is None:
                    wait()
                else:
                    pl.when(jnp.logical_or(source == me, got_it))(wait)

    farthest = sum(n - 1 for n in sizes) + 1

    def send_x(m):
        return pltpu.make_async_remote_copy(
            src_ref=xbuf.at[role, m],
            dst_ref=xbuf.at[role, m],
            send_sem=x_send.at[2, m],
            recv_sem=x_recv.at[1, m],
            device_id={"ctx": partner},
            device_id_type=MESH,
        )

    def pass_on(to, m):
        return pltpu.make_async_remote_copy(
            src_ref=result.at[m],
            dst_ref=xbuf.at[role, m],
            send_sem=x_send.at[to, m],
            recv_sem=x_recv.at[to, m],
            device_id={"section": lax.rem(section + 1, sections), "ctx": (me, partner)[to]},
            device_id_type=MESH,
        )

    def wait_x(which, m):
        place = role if which == 0 else 1 - role
        pltpu.make_async_remote_copy(
            src_ref=result.at[m],
            dst_ref=xbuf.at[place, m],
            send_sem=x_send.at[which, m],
            recv_sem=x_recv.at[which, m],
            device_id={"ctx": partner},
            device_id_type=MESH,
        ).wait_recv()

    send_decay = pltpu.make_async_remote_copy(
        src_ref=decay,
        dst_ref=decays,
        send_sem=d_sem.at[0],
        recv_sem=d_sem.at[1],
        device_id={"ctx": partner},
        device_id_type=MESH,
    )
    send_decay.start()
    for c in staged_a:
        c.wait()
    staged_b.wait()

    @pl.when(section > 0)
    def _():
        pl.semaphore_wait(start_sem, 1)

    for index in of(0):
        onward(me, mine, index, lambda c: c.start())

    @pl.when(section == 0)
    def _():
        x_own.wait()
        for m in range(micro):
            send_x(m).start()

    for index in of(1):
        onward(me, mine, index, lambda c: c.start())

    at_row = lax.broadcasted_iota(jnp.int32, (rows, rows), 0)
    at_col = lax.broadcasted_iota(jnp.int32, (rows, rows), 1)
    causal = at_row >= at_col
    upper = (at_row <= at_col).astype(f32)

    def accumulate(place, source):
        spread = (
            lax.broadcasted_iota(jnp.int32, (half_heads, half_heads * lanes), 0)
            == lax.broadcasted_iota(jnp.int32, (half_heads, half_heads * lanes), 1) // lanes
        ).astype(f32)
        for m in range(micro):
            own = source[m, pl.ds(pl.multiple_of(role * half_heads, half_heads), half_heads), :]
            summed = dot(own, upper, precision=lax.Precision.HIGHEST)
            cumt[place * micro + m] = summed
            cumx[place * micro + m] = dot(
                summed, spread, ((0,), (0,)), precision=lax.Precision.HIGHEST
            )

    accumulate(role, decay)
    send_decay.wait_recv()
    accumulate(1 - role, decays)

    def let_next_start():
        @pl.when(section < sections - 1)
        def _():
            pl.semaphore_signal(
                start_sem, inc=1, device_id={"section": section + 1}, device_id_type=MESH
            )

    def measure_rows(place, m):
        @pl.loop(0, rows // TILE)
        def _(q):
            at = pl.multiple_of(q * TILE, TILE)
            wide_rows = xbuf[place, m, pl.ds(at, TILE), :].astype(f32)
            scale = lax.rsqrt(jnp.mean(wide_rows * wide_rows, axis=-1, keepdims=True) + 1e-05)
            scales[place * micro + m, pl.ds(at, TILE), :] = jnp.broadcast_to(scale, (TILE, lanes))

    receive(0, 1, farthest)
    let_next_start()

    @pl.when(section > 0)
    def _():
        receive(1, 1, farthest)
        drain(0)

    def project(place):
        for m in range(micro):
            measure_rows(place, m)

        @pl.loop(0, 3 * half_inner // 256)
        def _(c):
            cols = pl.ds(pl.multiple_of(c * 256, 256), 256)
            inputs = xbuf[place].reshape(micro * rows, width)
            product = dot(inputs, full_a[role, :, cols])
            scale = jnp.concatenate(
                [scales[place * micro + m] for m in range(micro)], axis=0
            )
            scale = jnp.concatenate([scale] * (256 // lanes), axis=1)
            proj[place, :, cols] = (product * scale).astype(bf16)

    @pl.when(section > 0)
    def _():
        for m in range(micro):
            wait_x(0, m)

    project(role)
    for m in range(micro):
        wait_x(1, m)
    project(1 - role)

    first_half = lax.broadcasted_iota(jnp.int32, (rows, lanes), 1) < head_dim
    first_item = lax.broadcasted_iota(jnp.int32, (head_dim, lanes), 1) < head_dim
    per_pair = head_dim // part

    def located(u):
        g, p = lax.div(u, pairs), lax.rem(u, pairs)
        place, m = lax.div(g, micro), lax.rem(g, micro)
        span = pl.ds(pl.multiple_of(m * rows, TILE), rows)

        def column(which):
            return pl.ds(pl.multiple_of(which * half_inner + p * lanes, lanes), lanes)

        def cum(h):
            return cumx[g, :, pl.ds(pl.multiple_of((2 * p + h) * lanes, lanes), lanes)]

        return place, m, p, span, column, cum

    @pl.loop(0, 2 * micro * pairs)
    def _(u):
        place, m, p, span, column, cum = located(u)
        decayed = jnp.where(first_half, cum(0), cum(1))
        ending = decayed[rows - 1 :, :]
        scaled = (proj[place, span, column(1)].astype(f32) * jnp.exp(ending - decayed)).astype(bf16)
        state = dot(scaled, proj[place, span, column(2)], ((0,), (0,)))
        packed = jnp.where(first_item, state[:head_dim], state[head_dim:]).astype(bf16)
        weight = jnp.broadcast_to(jnp.exp(ending), (TILE, lanes)).astype(bf16)
        for piece in range(per_pair):
            to = (m * pairs + p) * per_pair + piece
            items[to, place, :part, :] = packed[piece * part : (piece + 1) * part]
            items[to, place, part:, :] = weight

    def first(to, slot_from):
        return pltpu.make_async_remote_copy(
            src_ref=items.at[to],
            dst_ref=got.at[slot_from],
            send_sem=s1.at[to],
            recv_sem=r1.at[slot_from],
            device_id={"ctx": device_of(to, role)},
            device_id_type=MESH,
        )

    def second(to, slot_from):
        return pltpu.make_async_remote_copy(
            src_ref=carried.at[to],
            dst_ref=landed.at[slot_from],
            send_sem=s2.at[to],
            recv_sem=r2.at[slot_from],
            device_id={"ctx": device_of(to, role)},
            device_id_type=MESH,
        )

    @pl.loop(1, peers)
    def _(k):
        first(lax.rem(my_peer + k, peers), my_peer).start()

    got[my_peer] = items[my_peer]

    def within(u):
        place, m, p, span, column, cum = located(u)
        queries, keys, values = (proj[place, span, column(i)] for i in range(3))
        outs = []
        for h in range(2):
            own_half = first_half if h == 0 else jnp.logical_not(first_half)
            scores = dot(jnp.where(own_half, queries, jnp.zeros_like(queries)), keys, ((1,), (1,)))
            gap = cum(h) - cumt[place * micro + m, pl.ds(2 * p + h, 1), :]
            weights = jnp.where(
                causal, scores * jnp.exp(jnp.where(causal, gap, 0.0)), 0.0
            ).astype(bf16)
            outs.append(dot(weights, values))
        intra[place, span, column(0)] = jnp.where(first_half, outs[0], outs[1])

    @pl.when(section == 0)
    def _():
        receive(1, 1, 2)

    @pl.loop(0, 2 * micro * pairs)
    def _(u):
        within(u)

    @pl.when(section == 0)
    def _():
        receive(1, 2, 3)

    def step(b, acc):
        peer = peer_of(b)
        side = lax.rem(lax.rem(lax.div(b, strides[axis]), sizes[axis]), 2)

        @pl.when(both(peer != my_peer, side == 0))
        def _():
            first(peer, peer).wait_recv()

        low = acc.astype(bf16)
        carried[peer, side] = low

        @pl.when(both(peer != my_peer, side == 1))
        def _():
            second(peer, my_peer).start()

        @pl.when(peer == my_peer)
        def _():
            landed[my_peer, side] = low

        item = got[peer, side].astype(f32)
        return acc * item[part : part + 1] + item[:part]

    lax.fori_loop(0, total, step, jnp.zeros((part, lanes), f32))

    @pl.when(section == 0)
    def _():
        receive(1, 3, farthest)

    @pl.loop(1, peers)
    def _(k):
        peer = lax.rem(my_peer + k, peers)
        second(peer, peer).wait_recv()

    def mix(u):
        place, m, p, span, column, cum = located(u)
        low = jnp.concatenate(
            [landed[(m * pairs + p) * per_pair + i, place] for i in range(per_pair)], axis=0
        )
        none = jnp.zeros_like(low)
        block = jnp.concatenate(
            [jnp.where(first_item, low, none), jnp.where(first_item, none, low)], axis=0
        )
        decayed = jnp.where(first_half, cum(0), cum(1))
        mixture = (
            intra[place, span, column(0)]
            + dot(proj[place, span, column(0)], block) * jnp.exp(decayed)
        )
        squares = mixture * mixture
        factors = [
            lax.rsqrt(
                jnp.sum(jnp.where(own, squares, 0.0), axis=-1, keepdims=True) / head_dim + 1e-05
            )
            for own in (first_half, jnp.logical_not(first_half))
        ]
        mixed[place, span, column(0)] = (
            mixture * jnp.where(first_half, factors[0], factors[1])
        ).astype(bf16)

    send_mixed = pltpu.make_async_remote_copy(
        src_ref=mixed.at[1 - role],
        dst_ref=mixed_in,
        send_sem=mix_sem.at[0],
        recv_sem=mix_sem.at[1],
        device_id={"ctx": partner},
        device_id_type=MESH,
    )

    @pl.loop(0, micro * pairs)
    def _(u):
        mix((1 - role) * (micro * pairs) + u)

    send_mixed.start()

    @pl.loop(0, micro * pairs)
    def _(u):
        mix(role * (micro * pairs) + u)

    send_mixed.wait_recv()

    @pl.loop(0, width // 256)
    def _(c):
        cols = pl.ds(pl.multiple_of(c * 256, 256), 256)
        here = pl.ds(pl.multiple_of(role * half_inner, TILE), half_inner)
        there = pl.ds(pl.multiple_of((1 - role) * half_inner, TILE), half_inner)
        product = dot(mixed[role], full_b[here, cols]) + dot(mixed_in[...], full_b[there, cols])
        for m in range(micro):
            result[m, :, cols] = (
                xbuf[role, m, :, cols].astype(f32) + product[m * rows : (m + 1) * rows]
            ).astype(bf16)

    @pl.when(section < sections - 1)
    def _():
        for m in range(micro):
            for to in range(2):
                pass_on(to, m).start()

    put = pltpu.make_async_copy(result, out, own_sem.at[1])
    put.start()

    @pl.when(section == 0)
    def _():
        drain(0)
        for m in range(micro):
            send_x(m).wait_send()

    drain(1)
    send_decay.wait_send()
    send_mixed.wait_send()

    @pl.loop(1, peers)
    def _(k):
        peer = lax.rem(my_peer + k, peers)
        first(peer, my_peer).wait_send()
        second(peer, my_peer).wait_send()

    put.wait()

    @pl.when(section < sections - 1)
    def _():
        for m in range(micro):
            for to in range(2):
                pass_on(to, m).wait_send()


def shards(sizes, sections, tokens, qkv_weight, out_weight, log_decay):
    micro, rows, width = tokens.shape
    total = int(np.prod(sizes))
    peers = total // 2
    heads = log_decay.shape[3]
    own = (qkv_weight[0], out_weight[0])
    inner = own[1].shape[0] * total
    half = inner // 2
    lanes = 2 * inner // heads
    part = micro * inner // 2 // total
    plan = [pieces(s.shape[0], sizes) for s in own]
    count = 2 * len(plan[0]) + len(plan[1])
    slots = sum(1 if s == 2 else 2 for s in sizes)
    f32, bf16 = jnp.float32, jnp.bfloat16
    dma = pltpu.SemaphoreType.DMA
    anywhere = pl.BlockSpec(memory_space=pl.ANY)
    vmem = pl.BlockSpec(memory_space=pltpu.VMEM)
    result = pl.pallas_call(
        functools.partial(whole_kernel, sizes, sections, plan, heads),
        out_shape=jax.ShapeDtypeStruct(tokens.shape, tokens.dtype),
        in_specs=[anywhere, vmem, anywhere, anywhere],
        out_specs=anywhere,
        scratch_shapes=[
            pltpu.VMEM((2, width, 3 * half), bf16),
            pltpu.VMEM((inner, width), bf16),
            pltpu.VMEM((2, micro, rows, width), bf16),
            pltpu.VMEM((2 * micro, rows, lanes), f32),
            pltpu.VMEM((2, micro * rows, 3 * half), bf16),
            pltpu.VMEM((micro, heads, rows), f32),
            pltpu.VMEM((2 * micro, rows, heads // 2 * lanes), f32),
            pltpu.VMEM((2 * micro, heads // 2, rows), f32),
            pltpu.VMEM((2, micro * rows, half), f32),
            pltpu.VMEM((2, micro * rows, half), bf16),
            pltpu.VMEM((micro * rows, half), bf16),
            pltpu.VMEM((micro, rows, width), bf16),
            pltpu.VMEM((peers, 2, part + TILE, lanes), bf16),
            pltpu.VMEM((peers, 2, part + TILE, lanes), bf16),
            pltpu.VMEM((peers, 2, part, lanes), bf16),
            pltpu.VMEM((peers, 2, part, lanes), bf16),
            dma((total, count, slots)),
            dma((total, count)),
            dma((8,)),
            dma((3, micro)),
            dma((2, micro)),
            dma((2,)),
            dma((2,)),
            pltpu.SemaphoreType.REGULAR,
            dma((peers,)),
            dma((peers,)),
            dma((peers,)),
            dma((peers,)),
        ],
        compiler_params=pltpu.CompilerParams(
            collective_id=0, has_side_effects=True, vmem_limit_bytes=60 * 2**20
        ),
        name="mixer_stack",
    )(tokens, jnp.swapaxes(log_decay[0], 1, 2), *own)
    return result[None]


def solution(mesh):
    in_specs = (
        P(None, "ctx", None),
        P("section", "ctx", None),
        P("section", "ctx", None),
        P("section", None, "ctx", None),
    )
    out_specs = P("section", None, "ctx", None)
    return jax.shard_map(
        functools.partial(shards, line_sizes(mesh), mesh.shape["section"]),
        mesh=mesh,
        in_specs=in_specs,
        out_specs=out_specs,
        check_vma=False,
    )
```

```python
import functools

import jax
import jax.numpy as jnp
import numpy as np
from jax import lax
from jax.experimental import pallas as pl
from jax.experimental.pallas import tpu as pltpu
from jax.sharding import PartitionSpec as P

MESH = pl.DeviceIdType.MESH
TILE = 16


def line_sizes(mesh):
    total = mesh.shape["ctx"]
    places = np.moveaxis(mesh.devices, mesh.axis_names.index("ctx"), 0).reshape(total, -1)[:, 0]
    sizes, left = [], total
    try:
        coords = [tuple(d.coords) for d in places]
    except AttributeError:
        coords = None
    if coords is not None:
        step = 1
        while step < total:
            changed = [a != b for a, b in zip(coords[0], coords[step])]
            axis = changed.index(True)
            size = 1
            while step * size < total and (
                size == 1 or (coords[step * size][axis] != coords[0][axis]
                and all(coords[step * size][i] == coords[0][i] for i in range(3) if i != axis))
            ):
                size += 1
            while total % (step * size):
                size -= 1
            sizes.insert(0, size)
            step *= size
    else:
        while left > 1:
            sizes.append(2)
            left //= 2
    return tuple(sizes)


def pair_axis(sizes):
    return next(i for i, s in enumerate(sizes) if s % 2 == 0)


def pieces(rows, sizes, parts):
    d, axis = len(sizes), pair_axis(sizes)
    rest = tuple(i for i in range(d) if i != axis)
    orders = [(axis,) + rest[::-1], (axis,) + rest]
    units = rows // TILE
    parts = min(parts, units)
    cuts = [units * p // parts * TILE for p in range(parts)] + [rows]
    return [(orders[p % 2], cuts[p], cuts[p + 1] - cuts[p]) for p in range(parts)]


def dot(a, b, contract=((1,), (0,)), precision=None):
    return lax.dot_general(
        a, b, (contract, ((), ())), precision=precision, preferred_element_type=jnp.float32
    )


def whole_kernel(
    sizes, sections, plan, heads, tokens, decay, shard_a, shard_b, out,
    full_a, full_b, relay_b, xbuf, scales, proj, decays, cumx, cumt, intra, mixed, mixed_in, result,
    items, got, carried, landed,
    send_sem, recv_sem, own_sem, x_send, x_recv, d_sem, mix_sem, hand_sem, whole_sem, start_sem, s1, r1, s2, r2,
):
    f32, bf16 = jnp.float32, jnp.bfloat16
    both = jnp.logical_and
    d = len(sizes)
    axis = pair_axis(sizes)
    total = int(np.prod(sizes))
    strides = [int(np.prod(sizes[i + 1 :])) for i in range(d)]
    me = lax.axis_index("ctx")
    section = lax.axis_index("section")

    def coords_of(index):
        return [lax.rem(lax.div(index, strides[i]), sizes[i]) for i in range(d)]

    mine = coords_of(me)
    role = lax.rem(mine[axis], 2)
    partner = me + (1 - 2 * role) * strides[axis]
    peers = total // 2
    wide = strides[axis] * sizes[axis]

    def peer_of(index):
        line = lax.rem(lax.div(index, strides[axis]), sizes[axis])
        return (
            lax.div(index, wide) * (wide // 2)
            + lax.div(line, 2) * strides[axis]
            + lax.rem(index, strides[axis])
        )

    def device_of(peer, side):
        line = lax.rem(lax.div(peer, strides[axis]), sizes[axis] // 2)
        return (
            lax.div(peer, wide // 2) * wide
            + (2 * line + side) * strides[axis]
            + lax.rem(peer, strides[axis])
        )

    my_peer = peer_of(me)

    ways = [(i, sign) for i in range(d) for sign in (1, -1)]
    most_ways = sum(min(n - 1, 2) for n in sizes)
    _, micro, rows, width = xbuf.shape
    half_inner = mixed.shape[2]
    half_heads = heads // 2
    head_dim = half_inner // half_heads
    pairs = half_heads // 2
    lanes = 2 * head_dim
    part = carried.shape[2]
    stripes = x_recv.shape[1]
    stripe = width // stripes
    depth_a, depth_b = shard_a.shape[0], shard_b.shape[0]

    staged_a = []
    for h in range(2):
        for which in range(3):
            staged_a.append(
                pltpu.make_async_copy(
                    shard_a.at[:, pl.ds((2 * which + h) * half_inner, half_inner)],
                    full_a.at[
                        h, pl.ds(pl.multiple_of(me * depth_a, TILE), depth_a),
                        pl.ds(which * half_inner, half_inner),
                    ],
                    own_sem.at[2 + 3 * h + which],
                )
            )
    staged_b = pltpu.make_async_copy(
        shard_b, full_b.at[pl.ds(pl.multiple_of(me * depth_b, TILE), depth_b)], own_sem.at[0]
    )
    x_own = pltpu.make_async_copy(tokens, xbuf.at[role], own_sem.at[1])
    for c in staged_a:
        c.start()
    staged_b.start()

    @pl.when(section == 0)
    def _():
        x_own.start()

    barrier = pltpu.get_barrier_semaphore()

    @pl.loop(1, total)
    def _(k):
        pl.semaphore_signal(
            barrier, inc=1, device_id={"ctx": lax.rem(me + k, total)}, device_id_type=MESH
        )

    sides = [1] if sections == 2 else [1, sections - 1]
    for away in sides:
        for chip in (me, partner):
            pl.semaphore_signal(
                barrier, inc=1,
                device_id={"section": lax.rem(section + away, sections), "ctx": chip},
                device_id_type=MESH,
            )

    pl.semaphore_wait(barrier, 2 * len(sides) + (total - 1))

    parts = [(0, h) + p for h in range(2) for p in plan[0]] + [(1, None) + p for p in plan[1]]

    def block(index, begin, size):
        a, h = parts[index][:2]
        return full_a.at[h, pl.ds(begin, size)] if a == 0 else relay_b.at[pl.ds(begin, size)]

    def copy(source, index, way):
        a, _, _, at, size = parts[index]
        i, sign = way
        target = block(
            index, pl.multiple_of(source * (depth_a, depth_b)[a] + at, TILE), size
        )
        return pltpu.make_async_remote_copy(
            src_ref=target,
            dst_ref=target,
            send_sem=send_sem.at[source, index],
            recv_sem=recv_sem.at[source, index],
            device_id={"ctx": me + sign * strides[i]},
            device_id_type=MESH,
        )

    def sent(source, index, times):
        target = block(index, 0, times * parts[index][4])
        return pltpu.make_async_remote_copy(
            src_ref=target,
            dst_ref=target,
            send_sem=send_sem.at[source, index],
            recv_sem=recv_sem.at[source, index],
            device_id={"ctx": partner},
            device_id_type=MESH,
        )

    def deliver(source, index):
        _, _, _, at, size = parts[index]
        span = pl.ds(pl.multiple_of(source * depth_b + at, TILE), size)
        return pltpu.make_async_remote_copy(
            src_ref=relay_b.at[span],
            dst_ref=full_b.at[span],
            send_sem=send_sem.at[source, index],
            recv_sem=whole_sem.at[0],
            device_id={"section": lax.rem(section + sections - 1, sections)},
            device_id_type=MESH,
        )

    def inside(i, place):
        return both(place >= 0, place < sizes[i])

    def goes(coords, index, way):
        h, order = parts[index][1:3]
        i, sign = way
        ok = both(inside(i, mine[i] + sign), (mine[i] - coords[i]) * sign >= 0)
        for later in order[order.index(i) + 1 :]:
            ok = both(ok, mine[later] == coords[later])
        if h is not None:
            if i == axis:
                ok = both(ok, jnp.logical_or(role != h, inside(i, mine[i] + 2 * sign)))
            else:
                ok = both(ok, role == h)
        return ok

    def onward(source, coords, index):
        for way in ways:
            @pl.when(goes(coords, index, way))
            def _(way=way):
                copy(source, index, way).start()

    def arrives(coords, index):
        h = parts[index][1]
        if h is None:
            return None
        gap = mine[axis] - coords[axis]
        beyond = jnp.where(gap > 0, inside(axis, mine[axis] + 1), inside(axis, mine[axis] - 1))
        ok = both(gap != 0, beyond)
        for i in range(d):
            if i != axis:
                ok = both(ok, mine[i] == coords[i])
        return jnp.logical_or(role == h, ok)

    def of(wanted):
        return [index for index in range(len(parts)) if parts[index][0] == wanted]

    def receive(wanted, least, most):
        @pl.loop(least * total, most * total)
        def _(k):
            hops, j = lax.div(k, total), lax.rem(k, total)
            source = lax.rem(me + j, total)
            coords = coords_of(source)
            away = sum(jnp.abs(mine[i] - coords[i]) for i in range(d))

            @pl.when(away == hops)
            def _():
                for index in of(wanted):
                    def take(index=index):
                        copy(source, index, ways[0]).wait_recv()
                        onward(source, coords, index)
                        if wanted == 1:
                            deliver(source, index).start()

                    ok = arrives(coords, index)
                    if ok is None:
                        take()
                    else:
                        pl.when(ok)(take)

    def drain(wanted):
        @pl.loop(0, total)
        def _(source):
            coords = coords_of(source)
            for index in of(wanted):
                times = sum(goes(coords, index, way).astype(jnp.int32) for way in ways)
                ok = arrives(coords, index)
                if ok is not None:
                    times = jnp.where(jnp.logical_or(source == me, ok), times, 0)
                if wanted == 1:
                    times = times + (source != me).astype(jnp.int32)
                for n in range(1, most_ways + 1 + wanted):
                    @pl.when(times == n)
                    def _(index=index, n=n):
                        sent(source, index, n).wait_send()

    farthest = sum(n - 1 for n in sizes) + 1

    def columns(c):
        return pl.ds(pl.multiple_of(c * stripe, stripe), stripe)

    def send_x(c):
        return pltpu.make_async_remote_copy(
            src_ref=xbuf.at[role, :, :, columns(c)],
            dst_ref=xbuf.at[role, :, :, columns(c)],
            send_sem=x_send.at[2, c],
            recv_sem=x_recv.at[1, c],
            device_id={"ctx": partner},
            device_id_type=MESH,
        )

    def pass_on(to, c):
        return pltpu.make_async_remote_copy(
            src_ref=result.at[:, :, columns(c)],
            dst_ref=xbuf.at[role, :, :, columns(c)],
            send_sem=x_send.at[to, c],
            recv_sem=x_recv.at[to, c],
            device_id={"section": lax.rem(section + 1, sections), "ctx": (me, partner)[to]},
            device_id_type=MESH,
        )

    def wait_x(which, c):
        place = role if which == 0 else 1 - role
        pltpu.make_async_remote_copy(
            src_ref=result.at[:, :, columns(c)],
            dst_ref=xbuf.at[place, :, :, columns(c)],
            send_sem=x_send.at[which, c],
            recv_sem=x_recv.at[which, c],
            device_id={"ctx": partner},
            device_id_type=MESH,
        ).wait_recv()

    hand = pltpu.make_async_remote_copy(
        src_ref=shard_b,
        dst_ref=relay_b.at[pl.ds(pl.multiple_of(me * depth_b, TILE), depth_b)],
        send_sem=hand_sem.at[0],
        recv_sem=hand_sem.at[1],
        device_id={"section": lax.rem(section + 1, sections)},
        device_id_type=MESH,
    )
    send_decay = pltpu.make_async_remote_copy(
        src_ref=decay,
        dst_ref=decays,
        send_sem=d_sem.at[0],
        recv_sem=d_sem.at[1],
        device_id={"ctx": partner},
        device_id_type=MESH,
    )
    send_decay.start()
    hand.start()
    for c in staged_a:
        c.wait()

    @pl.when(section == 0)
    def _():
        for index in of(0):
            onward(me, mine, index)
        x_own.wait()
        for c in range(stripes):
            send_x(c).start()

    staged_b.wait()

    at_row = lax.broadcasted_iota(jnp.int32, (rows, rows), 0)
    at_col = lax.broadcasted_iota(jnp.int32, (rows, rows), 1)
    causal = at_row >= at_col
    upper = (at_row <= at_col).astype(f32)

    def accumulate(place, source):
        spread = (
            lax.broadcasted_iota(jnp.int32, (half_heads, half_heads * lanes), 0)
            == lax.broadcasted_iota(jnp.int32, (half_heads, half_heads * lanes), 1) // lanes
        ).astype(f32)
        for m in range(micro):
            own = source[m, pl.ds(pl.multiple_of(role * half_heads, half_heads), half_heads), :]
            summed = dot(own, upper, precision=lax.Precision.HIGHEST)
            cumt[place * micro + m] = summed
            cumx[place * micro + m] = dot(
                summed, spread, ((0,), (0,)), precision=lax.Precision.HIGHEST
            )

    accumulate(role, decay)
    send_decay.wait_recv()
    accumulate(1 - role, decays)

    def let_next_start():
        @pl.when(section < sections - 1)
        def _():
            pl.semaphore_signal(
                start_sem, inc=1, device_id={"section": section + 1}, device_id_type=MESH
            )

    def measure_rows(place, m):
        @pl.loop(0, rows // TILE)
        def _(q):
            at = pl.multiple_of(q * TILE, TILE)
            wide_rows = xbuf[place, m, pl.ds(at, TILE), :].astype(f32)
            scale = lax.rsqrt(jnp.mean(wide_rows * wide_rows, axis=-1, keepdims=True) + 1e-05)
            scales[place * micro + m, pl.ds(at, TILE), :] = jnp.broadcast_to(scale, (TILE, lanes))

    def relay_own():
        hand.wait_recv()
        for index in of(1):
            onward(me, mine, index)

    @pl.when(section > 0)
    def _():
        pl.semaphore_wait(start_sem, 1)
        relay_own()
        receive(1, 1, 4)
        for index in of(0):
            onward(me, mine, index)
        receive(1, 4, farthest)

    receive(0, 1, 3)
    let_next_start()
    receive(0, 3, farthest)

    @pl.when(section > 0)
    def _():
        drain(1)
        drain(0)

    def project(place):
        for m in range(micro):
            measure_rows(place, m)

        @pl.loop(0, 3 * half_inner // 256)
        def _(c):
            cols = pl.ds(pl.multiple_of(c * 256, 256), 256)
            inputs = xbuf[place].reshape(micro * rows, width)
            product = dot(inputs, full_a[role, :, cols])
            scale = jnp.concatenate(
                [scales[place * micro + m] for m in range(micro)], axis=0
            )
            scale = jnp.concatenate([scale] * (256 // lanes), axis=1)
            proj[place, :, cols] = (product * scale).astype(bf16)

    @pl.when(section > 0)
    def _():
        for c in range(stripes):
            wait_x(0, c)

    project(role)
    for c in range(stripes):
        wait_x(1, c)
    project(1 - role)

    first_half = lax.broadcasted_iota(jnp.int32, (rows, lanes), 1) < head_dim
    first_item = lax.broadcasted_iota(jnp.int32, (head_dim, lanes), 1) < head_dim
    per_pair = head_dim // part

    def located(u):
        g, p = lax.div(u, pairs), lax.rem(u, pairs)
        place, m = lax.div(g, micro), lax.rem(g, micro)
        span = pl.ds(pl.multiple_of(m * rows, TILE), rows)

        def column(which):
            return pl.ds(pl.multiple_of(which * half_inner + p * lanes, lanes), lanes)

        def cum(h):
            return cumx[g, :, pl.ds(pl.multiple_of((2 * p + h) * lanes, lanes), lanes)]

        return place, m, p, span, column, cum

    @pl.loop(0, 2 * micro * pairs)
    def _(u):
        place, m, p, span, column, cum = located(u)
        decayed = jnp.where(first_half, cum(0), cum(1))
        ending = decayed[rows - 1 :, :]
        scaled = (proj[place, span, column(1)].astype(f32) * jnp.exp(ending - decayed)).astype(bf16)
        state = dot(scaled, proj[place, span, column(2)], ((0,), (0,)))
        packed = jnp.where(first_item, state[:head_dim], state[head_dim:]).astype(bf16)
        weight = jnp.broadcast_to(jnp.exp(ending), (TILE, lanes)).astype(bf16)
        for piece in range(per_pair):
            to = (m * pairs + p) * per_pair + piece
            items[to, place, :part, :] = packed[piece * part : (piece + 1) * part]
            items[to, place, part:, :] = weight

    def first(to, slot_from):
        return pltpu.make_async_remote_copy(
            src_ref=items.at[to],
            dst_ref=got.at[slot_from],
            send_sem=s1.at[to],
            recv_sem=r1.at[slot_from],
            device_id={"ctx": device_of(to, role)},
            device_id_type=MESH,
        )

    def second(to, slot_from):
        return pltpu.make_async_remote_copy(
            src_ref=carried.at[to],
            dst_ref=landed.at[slot_from],
            send_sem=s2.at[to],
            recv_sem=r2.at[slot_from],
            device_id={"ctx": device_of(to, role)},
            device_id_type=MESH,
        )

    @pl.loop(1, peers)
    def _(k):
        first(lax.rem(my_peer + k, peers), my_peer).start()

    got[my_peer] = items[my_peer]

    def within(u):
        place, m, p, span, column, cum = located(u)
        queries, keys, values = (proj[place, span, column(i)] for i in range(3))
        outs = []
        for h in range(2):
            own_half = first_half if h == 0 else jnp.logical_not(first_half)
            scores = dot(jnp.where(own_half, queries, jnp.zeros_like(queries)), keys, ((1,), (1,)))
            gap = cum(h) - cumt[place * micro + m, pl.ds(2 * p + h, 1), :]
            weights = jnp.where(
                causal, scores * jnp.exp(jnp.where(causal, gap, 0.0)), 0.0
            ).astype(bf16)
            outs.append(dot(weights, values))
        intra[place, span, column(0)] = jnp.where(first_half, outs[0], outs[1])

    @pl.loop(0, 2 * micro * pairs)
    def _(u):
        within(u)

    def step(b, acc):
        peer = peer_of(b)
        side = lax.rem(lax.rem(lax.div(b, strides[axis]), sizes[axis]), 2)

        @pl.when(both(peer != my_peer, side == 0))
        def _():
            first(peer, peer).wait_recv()

        low = acc.astype(bf16)
        carried[peer, side] = low

        @pl.when(both(peer != my_peer, side == 1))
        def _():
            second(peer, my_peer).start()

        @pl.when(peer == my_peer)
        def _():
            landed[my_peer, side] = low

        item = got[peer, side].astype(f32)
        return acc * item[part : part + 1] + item[:part]

    lax.fori_loop(0, total, step, jnp.zeros((part, lanes), f32))

    @pl.loop(1, peers)
    def _(k):
        peer = lax.rem(my_peer + k, peers)
        second(peer, peer).wait_recv()

    def mix(u):
        place, m, p, span, column, cum = located(u)
        low = jnp.concatenate(
            [landed[(m * pairs + p) * per_pair + i, place] for i in range(per_pair)], axis=0
        )
        none = jnp.zeros_like(low)
        block = jnp.concatenate(
            [jnp.where(first_item, low, none), jnp.where(first_item, none, low)], axis=0
        )
        decayed = jnp.where(first_half, cum(0), cum(1))
        mixture = (
            intra[place, span, column(0)]
            + dot(proj[place, span, column(0)], block) * jnp.exp(decayed)
        )
        squares = mixture * mixture
        factors = [
            lax.rsqrt(
                jnp.sum(jnp.where(own, squares, 0.0), axis=-1, keepdims=True) / head_dim + 1e-05
            )
            for own in (first_half, jnp.logical_not(first_half))
        ]
        mixed[place, span, column(0)] = (
            mixture * jnp.where(first_half, factors[0], factors[1])
        ).astype(bf16)

    send_mixed = pltpu.make_async_remote_copy(
        src_ref=mixed.at[1 - role],
        dst_ref=mixed_in,
        send_sem=mix_sem.at[0],
        recv_sem=mix_sem.at[1],
        device_id={"ctx": partner},
        device_id_type=MESH,
    )

    @pl.loop(0, micro * pairs)
    def _(u):
        mix((1 - role) * (micro * pairs) + u)

    send_mixed.start()

    @pl.loop(0, micro * pairs)
    def _(u):
        mix(role * (micro * pairs) + u)

    send_mixed.wait_recv()

    pltpu.make_async_remote_copy(
        src_ref=full_b.at[pl.ds(0, (total - 1) * depth_b)],
        dst_ref=full_b.at[pl.ds(0, (total - 1) * depth_b)],
        send_sem=hand_sem.at[0],
        recv_sem=whole_sem.at[0],
        device_id={"section": lax.rem(section + sections - 1, sections)},
        device_id_type=MESH,
    ).wait_recv()

    here = pl.ds(pl.multiple_of(role * half_inner, TILE), half_inner)
    there = pl.ds(pl.multiple_of((1 - role) * half_inner, TILE), half_inner)

    @pl.loop(0, stripes)
    def _(c):
        for piece in range(stripe // 256):
            cols = pl.ds(pl.multiple_of(c * stripe + piece * 256, 256), 256)
            product = dot(mixed[role], full_b[here, cols]) + dot(mixed_in[...], full_b[there, cols])
            for m in range(micro):
                result[m, :, cols] = (
                    xbuf[role, m, :, cols].astype(f32) + product[m * rows : (m + 1) * rows]
                ).astype(bf16)

        @pl.when(section < sections - 1)
        def _():
            for to in (1, 0):
                pass_on(to, c).start()

    put = pltpu.make_async_copy(result, out, own_sem.at[1])
    put.start()

    @pl.when(section == 0)
    def _():
        relay_own()
        receive(1, 1, farthest)
        drain(0)
        drain(1)
        for c in range(stripes):
            send_x(c).wait_send()

    hand.wait_send()
    send_decay.wait_send()
    send_mixed.wait_send()

    @pl.loop(1, peers)
    def _(k):
        peer = lax.rem(my_peer + k, peers)
        first(peer, my_peer).wait_send()
        second(peer, my_peer).wait_send()

    put.wait()

    @pl.when(section < sections - 1)
    def _():
        for c in range(stripes):
            for to in range(2):
                pass_on(to, c).wait_send()


def shards(sizes, sections, tokens, qkv_weight, out_weight, log_decay):
    micro, rows, width = tokens.shape
    total = int(np.prod(sizes))
    peers = total // 2
    heads = log_decay.shape[3]
    own = (qkv_weight[0], out_weight[0])
    inner = own[1].shape[0] * total
    half = inner // 2
    lanes = 2 * inner // heads
    part = micro * inner // 2 // total
    plan = [pieces(s.shape[0], sizes, n) for s, n in zip(own, (2, 2))]
    count = 2 * len(plan[0]) + len(plan[1])
    stripes = max(1, width // 512)
    f32, bf16 = jnp.float32, jnp.bfloat16
    dma = pltpu.SemaphoreType.DMA
    anywhere = pl.BlockSpec(memory_space=pl.ANY)
    vmem = pl.BlockSpec(memory_space=pltpu.VMEM)
    result = pl.pallas_call(
        functools.partial(whole_kernel, sizes, sections, plan, heads),
        out_shape=jax.ShapeDtypeStruct(tokens.shape, tokens.dtype),
        in_specs=[anywhere, vmem, anywhere, anywhere],
        out_specs=anywhere,
        scratch_shapes=[
            pltpu.VMEM((2, width, 3 * half), bf16),
            pltpu.VMEM((inner, width), bf16),
            pltpu.VMEM((inner, width), bf16),
            pltpu.VMEM((2, micro, rows, width), bf16),
            pltpu.VMEM((2 * micro, rows, lanes), f32),
            pltpu.VMEM((2, micro * rows, 3 * half), bf16),
            pltpu.VMEM((micro, heads, rows), f32),
            pltpu.VMEM((2 * micro, rows, heads // 2 * lanes), f32),
            pltpu.VMEM((2 * micro, heads // 2, rows), f32),
            pltpu.VMEM((2, micro * rows, half), f32),
            pltpu.VMEM((2, micro * rows, half), bf16),
            pltpu.VMEM((micro * rows, half), bf16),
            pltpu.VMEM((micro, rows, width), bf16),
            pltpu.VMEM((peers, 2, part + TILE, lanes), bf16),
            pltpu.VMEM((peers, 2, part + TILE, lanes), bf16),
            pltpu.VMEM((peers, 2, part, lanes), bf16),
            pltpu.VMEM((peers, 2, part, lanes), bf16),
            dma((total, count)),
            dma((total, count)),
            dma((8,)),
            dma((3, stripes)),
            dma((2, stripes)),
            dma((2,)),
            dma((2,)),
            dma((2,)),
            dma((1,)),
            pltpu.SemaphoreType.REGULAR,
            dma((peers,)),
            dma((peers,)),
            dma((peers,)),
            dma((peers,)),
        ],
        compiler_params=pltpu.CompilerParams(
            collective_id=0, has_side_effects=True, vmem_limit_bytes=60 * 2**20
        ),
        name="mixer_stack",
    )(tokens, jnp.swapaxes(log_decay[0], 1, 2), *own)
    return result[None]


def solution(mesh):
    in_specs = (
        P(None, "ctx", None),
        P("section", "ctx", None),
        P("section", "ctx", None),
        P("section", None, "ctx", None),
    )
    out_specs = P("section", None, "ctx", None)
    return jax.shard_map(
        functools.partial(shards, line_sizes(mesh), mesh.shape["section"]),
        mesh=mesh,
        in_specs=in_specs,
        out_specs=out_specs,
        check_vma=False,
    )
```

```python
import functools

import jax
import jax.numpy as jnp
import numpy as np
from jax import lax
from jax.experimental import pallas as pl
from jax.experimental.pallas import tpu as pltpu
from jax.sharding import PartitionSpec as P

MESH = pl.DeviceIdType.MESH
TILE = 16


def line_sizes(mesh):
    total = mesh.shape["ctx"]
    places = np.moveaxis(mesh.devices, mesh.axis_names.index("ctx"), 0).reshape(total, -1)[:, 0]
    sizes, left = [], total
    try:
        coords = [tuple(d.coords) for d in places]
    except AttributeError:
        coords = None
    if coords is not None:
        step = 1
        while step < total:
            changed = [a != b for a, b in zip(coords[0], coords[step])]
            axis = changed.index(True)
            size = 1
            while step * size < total and (
                size == 1 or (coords[step * size][axis] != coords[0][axis]
                and all(coords[step * size][i] == coords[0][i] for i in range(3) if i != axis))
            ):
                size += 1
            while total % (step * size):
                size -= 1
            sizes.insert(0, size)
            step *= size
    else:
        while left > 1:
            sizes.append(2)
            left //= 2
    return tuple(sizes)


def pair_axis(sizes):
    return next(i for i, s in enumerate(sizes) if s % 2 == 0)


def pieces(rows, sizes, parts):
    d, axis = len(sizes), pair_axis(sizes)
    rest = tuple(i for i in range(d) if i != axis)
    orders = [(axis,) + rest[::-1], (axis,) + rest]
    units = rows // TILE
    parts = min(parts, units)
    cuts = [units * p // parts * TILE for p in range(parts)] + [rows]
    return [(orders[p % 2], cuts[p], cuts[p + 1] - cuts[p]) for p in range(parts)]


def place_in_line(me, size, t):
    low = jnp.minimum(me, size - 1 - me)
    half = lax.div(t + 1, 2)
    near = jnp.where(lax.rem(t, 2) == 1, me + half, me - half)
    far = jnp.where(me < size - 1 - me, me + (t - low), me - (t - low))
    return jnp.where(t <= 2 * low, near, far)


def dot(a, b, contract=((1,), (0,)), precision=None):
    return lax.dot_general(
        a, b, (contract, ((), ())), precision=precision, preferred_element_type=jnp.float32
    )


def whole_kernel(
    sizes, sections, plan, heads, tokens, decay, shard_a, shard_b, out,
    full_a, full_b, relay_b, xbuf, scales, proj, decays, cumx, cumt, intra, mixed, mixed_in, result,
    items, got, carried, landed,
    send_sem, recv_sem, own_sem, x_send, x_recv, put_sem, d_sem, mix_sem, hand_sem, whole_sem, start_sem, s1, r1, s2, r2,
):
    f32, bf16 = jnp.float32, jnp.bfloat16
    both = jnp.logical_and
    d = len(sizes)
    axis = pair_axis(sizes)
    total = int(np.prod(sizes))
    strides = [int(np.prod(sizes[i + 1 :])) for i in range(d)]
    me = lax.axis_index("ctx")
    section = lax.axis_index("section")

    def coords_of(index):
        return [lax.rem(lax.div(index, strides[i]), sizes[i]) for i in range(d)]

    mine = coords_of(me)
    role = lax.rem(mine[axis], 2)
    partner = me + (1 - 2 * role) * strides[axis]
    peers = total // 2
    wide = strides[axis] * sizes[axis]

    def peer_of(index):
        line = lax.rem(lax.div(index, strides[axis]), sizes[axis])
        return (
            lax.div(index, wide) * (wide // 2)
            + lax.div(line, 2) * strides[axis]
            + lax.rem(index, strides[axis])
        )

    def device_of(peer, side):
        line = lax.rem(lax.div(peer, strides[axis]), sizes[axis] // 2)
        return (
            lax.div(peer, wide // 2) * wide
            + (2 * line + side) * strides[axis]
            + lax.rem(peer, strides[axis])
        )

    my_peer = peer_of(me)

    ways = [(i, sign) for i in range(d) for sign in (1, -1)]
    most_ways = sum(min(n - 1, 2) for n in sizes)
    _, micro, rows, width = xbuf.shape
    half_inner = mixed.shape[2]
    half_heads = heads // 2
    head_dim = half_inner // half_heads
    pairs = half_heads // 2
    lanes = 2 * head_dim
    part = carried.shape[2]
    stripes = x_recv.shape[1]
    stripe = width // stripes
    depth_a, depth_b = shard_a.shape[0], shard_b.shape[0]

    staged_a = []
    for h in range(2):
        for which in range(3):
            staged_a.append(
                pltpu.make_async_copy(
                    shard_a.at[:, pl.ds((2 * which + h) * half_inner, half_inner)],
                    full_a.at[
                        h, pl.ds(pl.multiple_of(me * depth_a, TILE), depth_a),
                        pl.ds(which * half_inner, half_inner),
                    ],
                    own_sem.at[2 + 3 * h + which],
                )
            )
    staged_b = pltpu.make_async_copy(
        shard_b, full_b.at[pl.ds(pl.multiple_of(me * depth_b, TILE), depth_b)], own_sem.at[0]
    )
    x_own = pltpu.make_async_copy(tokens, xbuf.at[role], own_sem.at[1])
    for c in staged_a:
        c.start()
    staged_b.start()

    @pl.when(section == 0)
    def _():
        x_own.start()

    barrier = pltpu.get_barrier_semaphore()

    @pl.loop(1, total)
    def _(k):
        pl.semaphore_signal(
            barrier, inc=1, device_id={"ctx": lax.rem(me + k, total)}, device_id_type=MESH
        )

    sides = [1] if sections == 2 else [1, sections - 1]
    for away in sides:
        for chip in (me, partner):
            pl.semaphore_signal(
                barrier, inc=1,
                device_id={"section": lax.rem(section + away, sections), "ctx": chip},
                device_id_type=MESH,
            )

    pl.semaphore_wait(barrier, 2 * len(sides) + (total - 1))

    parts = [(0, h) + p for h in range(2) for p in plan[0]] + [(1, None) + p for p in plan[1]]

    def block(index, begin, size):
        a, h = parts[index][:2]
        return full_a.at[h, pl.ds(begin, size)] if a == 0 else relay_b.at[pl.ds(begin, size)]

    def copy(source, index, way):
        a, _, _, at, size = parts[index]
        i, sign = way
        target = block(
            index, pl.multiple_of(source * (depth_a, depth_b)[a] + at, TILE), size
        )
        return pltpu.make_async_remote_copy(
            src_ref=target,
            dst_ref=target,
            send_sem=send_sem.at[source, index],
            recv_sem=recv_sem.at[source, index],
            device_id={"ctx": me + sign * strides[i]},
            device_id_type=MESH,
        )

    def sent(source, index, times):
        target = block(index, 0, times * parts[index][4])
        return pltpu.make_async_remote_copy(
            src_ref=target,
            dst_ref=target,
            send_sem=send_sem.at[source, index],
            recv_sem=recv_sem.at[source, index],
            device_id={"ctx": partner},
            device_id_type=MESH,
        )

    def deliver(source, index):
        _, _, _, at, size = parts[index]
        span = pl.ds(pl.multiple_of(source * depth_b + at, TILE), size)
        return pltpu.make_async_remote_copy(
            src_ref=relay_b.at[span],
            dst_ref=full_b.at[span],
            send_sem=send_sem.at[source, index],
            recv_sem=whole_sem.at[0],
            device_id={"section": lax.rem(section + sections - 1, sections)},
            device_id_type=MESH,
        )

    def inside(i, place):
        return both(place >= 0, place < sizes[i])

    def goes(coords, index, way):
        h, order = parts[index][1:3]
        i, sign = way
        ok = both(inside(i, mine[i] + sign), (mine[i] - coords[i]) * sign >= 0)
        for later in order[order.index(i) + 1 :]:
            ok = both(ok, mine[later] == coords[later])
        if h is not None:
            if i == axis:
                ok = both(ok, jnp.logical_or(role != h, inside(i, mine[i] + 2 * sign)))
            else:
                ok = both(ok, role == h)
        return ok

    def onward(source, coords, index):
        for way in ways:
            @pl.when(goes(coords, index, way))
            def _(way=way):
                copy(source, index, way).start()

    def arrives(coords, index):
        h = parts[index][1]
        if h is None:
            return None
        gap = mine[axis] - coords[axis]
        beyond = jnp.where(gap > 0, inside(axis, mine[axis] + 1), inside(axis, mine[axis] - 1))
        ok = both(gap != 0, beyond)
        for i in range(d):
            if i != axis:
                ok = both(ok, mine[i] == coords[i])
        return jnp.logical_or(role == h, ok)

    def of(wanted):
        return [index for index in range(len(parts)) if parts[index][0] == wanted]

    def source_of(j):
        coords = coords_of(j)
        for i in range(d):
            if i == axis:
                coords[i] = place_in_line(mine[i], sizes[i], sizes[i] - 1 - coords[i])
            else:
                coords[i] = lax.rem(mine[i] + coords[i], sizes[i])
        return sum(c * s for c, s in zip(coords, strides)), coords

    def receive(wanted, least, most):
        @pl.loop(least * total, most * total)
        def _(k):
            hops, j = lax.div(k, total), lax.rem(k, total)
            source, coords = source_of(j)
            away = sum(jnp.abs(mine[i] - coords[i]) for i in range(d))

            @pl.when(away == hops)
            def _():
                for index in of(wanted):
                    def take(index=index):
                        copy(source, index, ways[0]).wait_recv()
                        onward(source, coords, index)
                        if wanted == 1:
                            deliver(source, index).start()

                    ok = arrives(coords, index)
                    if ok is None:
                        take()
                    else:
                        pl.when(ok)(take)

    def drain(wanted):
        @pl.loop(0, total)
        def _(source):
            coords = coords_of(source)
            for index in of(wanted):
                times = sum(goes(coords, index, way).astype(jnp.int32) for way in ways)
                ok = arrives(coords, index)
                if ok is not None:
                    times = jnp.where(jnp.logical_or(source == me, ok), times, 0)
                if wanted == 1:
                    times = times + (source != me).astype(jnp.int32)
                for n in range(1, most_ways + 1 + wanted):
                    @pl.when(times == n)
                    def _(index=index, n=n):
                        sent(source, index, n).wait_send()

    farthest = sum(n - 1 for n in sizes) + 1

    def columns(c):
        return pl.ds(pl.multiple_of(c * stripe, stripe), stripe)

    def send_x(c):
        return pltpu.make_async_remote_copy(
            src_ref=xbuf.at[role, :, :, columns(c)],
            dst_ref=xbuf.at[role, :, :, columns(c)],
            send_sem=x_send.at[2, c],
            recv_sem=x_recv.at[1, c],
            device_id={"ctx": partner},
            device_id_type=MESH,
        )

    def pass_on(to, c):
        return pltpu.make_async_remote_copy(
            src_ref=result.at[:, :, columns(c)],
            dst_ref=xbuf.at[role, :, :, columns(c)],
            send_sem=x_send.at[to, c],
            recv_sem=x_recv.at[to, c],
            device_id={"section": lax.rem(section + 1, sections), "ctx": (me, partner)[to]},
            device_id_type=MESH,
        )

    def wait_x(which, c):
        place = role if which == 0 else 1 - role
        pltpu.make_async_remote_copy(
            src_ref=result.at[:, :, columns(c)],
            dst_ref=xbuf.at[place, :, :, columns(c)],
            send_sem=x_send.at[which, c],
            recv_sem=x_recv.at[which, c],
            device_id={"ctx": partner},
            device_id_type=MESH,
        ).wait_recv()

    def put(c):
        return pltpu.make_async_copy(
            result.at[:, :, columns(c)], out.at[:, :, columns(c)], put_sem.at[c]
        )

    hand = pltpu.make_async_remote_copy(
        src_ref=shard_b,
        dst_ref=relay_b.at[pl.ds(pl.multiple_of(me * depth_b, TILE), depth_b)],
        send_sem=hand_sem.at[0],
        recv_sem=hand_sem.at[1],
        device_id={"section": lax.rem(section + 1, sections)},
        device_id_type=MESH,
    )
    send_decay = pltpu.make_async_remote_copy(
        src_ref=decay,
        dst_ref=decays,
        send_sem=d_sem.at[0],
        recv_sem=d_sem.at[1],
        device_id={"ctx": partner},
        device_id_type=MESH,
    )
    send_decay.start()
    hand.start()
    for c in staged_a:
        c.wait()

    @pl.when(section == 0)
    def _():
        for index in of(0):
            onward(me, mine, index)
        x_own.wait()

    staged_b.wait()

    at_row = lax.broadcasted_iota(jnp.int32, (rows, rows), 0)
    at_col = lax.broadcasted_iota(jnp.int32, (rows, rows), 1)
    causal = at_row >= at_col
    upper = (at_row <= at_col).astype(f32)

    def accumulate(place, source):
        spread = (
            lax.broadcasted_iota(jnp.int32, (half_heads, half_heads * lanes), 0)
            == lax.broadcasted_iota(jnp.int32, (half_heads, half_heads * lanes), 1) // lanes
        ).astype(f32)
        for m in range(micro):
            own = source[m, pl.ds(pl.multiple_of(role * half_heads, half_heads), half_heads), :]
            summed = dot(own, upper, precision=lax.Precision.HIGHEST)
            cumt[place * micro + m] = summed
            cumx[place * micro + m] = dot(
                summed, spread, ((0,), (0,)), precision=lax.Precision.HIGHEST
            )

    accumulate(role, decay)
    send_decay.wait_recv()
    accumulate(1 - role, decays)

    def let_next_start():
        pl.semaphore_signal(
            start_sem, inc=1, device_id={"section": lax.rem(section + 1, sections)},
            device_id_type=MESH,
        )

    def measure_rows(place, m):
        @pl.loop(0, rows // TILE, unroll=4)
        def _(q):
            at = pl.multiple_of(q * TILE, TILE)
            wide_rows = xbuf[place, m, pl.ds(at, TILE), :].astype(f32)
            scale = lax.rsqrt(jnp.mean(wide_rows * wide_rows, axis=-1, keepdims=True) + 1e-05)
            scales[place * micro + m, pl.ds(at, TILE), :] = jnp.broadcast_to(scale, (TILE, lanes))

    def relay_own():
        hand.wait_recv()
        for index in of(1):
            onward(me, mine, index)

    def send_stripes(least, most):
        @pl.when(section == 0)
        def _():
            for c in range(least, most):
                send_x(c).start()

    @pl.when(section > 0)
    def _():
        pl.semaphore_wait(start_sem, 1)
        relay_own()
        receive(1, 1, 3)
        for index in of(0):
            onward(me, mine, index)
        receive(1, 3, 4)
        receive(0, 1, 2)
        receive(1, 4, 5)
        receive(0, 2, 3)
        let_next_start()
        receive(1, 5, farthest)
        receive(0, 3, farthest - 1)
        for c in range(stripes):
            wait_x(0, c)
        for m in range(micro):
            measure_rows(role, m)
        for c in range(stripes):
            wait_x(1, c)
        for m in range(micro):
            measure_rows(1 - role, m)
        receive(0, farthest - 1, farthest)

    @pl.when(section == 0)
    def _():
        receive(0, 1, 2)
        send_stripes(0, stripes * 2 // 4)
        receive(0, 2, 3)
        send_stripes(stripes * 2 // 4, stripes * 3 // 4)
        let_next_start()
        receive(0, 3, 4)
        send_stripes(stripes * 3 // 4, stripes)
        for m in range(micro):
            measure_rows(role, m)
        receive(0, 4, farthest - 1)
        for c in range(stripes):
            wait_x(1, c)
        for m in range(micro):
            measure_rows(1 - role, m)
        receive(0, farthest - 1, farthest)

    def project(place):
        @pl.loop(0, 3 * half_inner // 512)
        def _(c):
            cols = pl.ds(pl.multiple_of(c * 512, 512), 512)
            inputs = xbuf[place].reshape(micro * rows, width)
            product = dot(inputs, full_a[role, :, cols])
            scale = jnp.concatenate(
                [scales[place * micro + m] for m in range(micro)], axis=0
            )
            scale = jnp.concatenate([scale] * (512 // lanes), axis=1)
            proj[place, :, cols] = (product * scale).astype(bf16)

    project(role)
    project(1 - role)

    first_half = lax.broadcasted_iota(jnp.int32, (rows, lanes), 1) < head_dim
    first_item = lax.broadcasted_iota(jnp.int32, (head_dim, lanes), 1) < head_dim
    per_pair = head_dim // part

    def located(u):
        g, p = lax.div(u, pairs), lax.rem(u, pairs)
        place, m = lax.div(g, micro), lax.rem(g, micro)
        span = pl.ds(pl.multiple_of(m * rows, TILE), rows)

        def column(which):
            return pl.ds(pl.multiple_of(which * half_inner + p * lanes, lanes), lanes)

        def cum(h):
            return cumx[g, :, pl.ds(pl.multiple_of((2 * p + h) * lanes, lanes), lanes)]

        return place, m, p, span, column, cum

    @pl.loop(0, 2 * micro * pairs, unroll=4)
    def _(u):
        place, m, p, span, column, cum = located(u)
        decayed = jnp.where(first_half, cum(0), cum(1))
        ending = decayed[rows - 1 :, :]
        scaled = (proj[place, span, column(1)].astype(f32) * jnp.exp(ending - decayed)).astype(bf16)
        state = dot(scaled, proj[place, span, column(2)], ((0,), (0,)))
        packed = jnp.where(first_item, state[:head_dim], state[head_dim:]).astype(bf16)
        weight = jnp.broadcast_to(jnp.exp(ending), (TILE, lanes)).astype(bf16)
        for piece in range(per_pair):
            to = (m * pairs + p) * per_pair + piece
            items[to, place, :part, :] = packed[piece * part : (piece + 1) * part]
            items[to, place, part:, :] = weight

    def first(to, slot_from):
        return pltpu.make_async_remote_copy(
            src_ref=items.at[to],
            dst_ref=got.at[slot_from],
            send_sem=s1.at[to],
            recv_sem=r1.at[slot_from],
            device_id={"ctx": device_of(to, role)},
            device_id_type=MESH,
        )

    def second(to, slot_from):
        return pltpu.make_async_remote_copy(
            src_ref=carried.at[to],
            dst_ref=landed.at[slot_from],
            send_sem=s2.at[to],
            recv_sem=r2.at[slot_from],
            device_id={"ctx": device_of(to, role)},
            device_id_type=MESH,
        )

    @pl.loop(1, peers)
    def _(k):
        first(lax.rem(my_peer + k, peers), my_peer).start()

    got[my_peer] = items[my_peer]

    def within(u):
        place, m, p, span, column, cum = located(u)
        queries, keys, values = (proj[place, span, column(i)] for i in range(3))
        outs = []
        for h in range(2):
            own_half = first_half if h == 0 else jnp.logical_not(first_half)
            scores = dot(jnp.where(own_half, queries, jnp.zeros_like(queries)), keys, ((1,), (1,)))
            gap = cum(h) - cumt[place * micro + m, pl.ds(2 * p + h, 1), :]
            weights = jnp.where(
                causal, scores * jnp.exp(jnp.where(causal, gap, 0.0)), 0.0
            ).astype(bf16)
            outs.append(dot(weights, values))
        intra[place, span, column(0)] = jnp.where(first_half, outs[0], outs[1])

    @pl.loop(0, micro * pairs, unroll=4)
    def _(u):
        within((1 - role) * (micro * pairs) + u)

    def step(b, acc):
        peer = peer_of(b)
        side = lax.rem(lax.rem(lax.div(b, strides[axis]), sizes[axis]), 2)

        @pl.when(both(peer != my_peer, side == 0))
        def _():
            first(peer, peer).wait_recv()

        low = acc.astype(bf16)
        carried[peer, side] = low

        @pl.when(both(peer != my_peer, side == 1))
        def _():
            second(peer, my_peer).start()

        @pl.when(peer == my_peer)
        def _():
            landed[my_peer, side] = low

        item = got[peer, side].astype(f32)
        return acc * item[part : part + 1] + item[:part]

    @pl.when(section > 0)
    def _():
        drain(0)

    lax.fori_loop(0, total, step, jnp.zeros((part, lanes), f32))

    @pl.loop(0, micro * pairs, unroll=4)
    def _(u):
        within(role * (micro * pairs) + u)

    @pl.when(section > 0)
    def _():
        drain(1)

    @pl.loop(1, peers)
    def _(k):
        peer = lax.rem(my_peer + k, peers)
        second(peer, peer).wait_recv()

    def mix(u):
        place, m, p, span, column, cum = located(u)
        low = jnp.concatenate(
            [landed[(m * pairs + p) * per_pair + i, place] for i in range(per_pair)], axis=0
        )
        none = jnp.zeros_like(low)
        block = jnp.concatenate(
            [jnp.where(first_item, low, none), jnp.where(first_item, none, low)], axis=0
        )
        decayed = jnp.where(first_half, cum(0), cum(1))
        mixture = (
            intra[place, span, column(0)]
            + dot(proj[place, span, column(0)], block) * jnp.exp(decayed)
        )
        squares = mixture * mixture
        factors = [
            lax.rsqrt(
                jnp.sum(jnp.where(own, squares, 0.0), axis=-1, keepdims=True) / head_dim + 1e-05
            )
            for own in (first_half, jnp.logical_not(first_half))
        ]
        mixed[place, span, column(0)] = (
            mixture * jnp.where(first_half, factors[0], factors[1])
        ).astype(bf16)

    send_mixed = pltpu.make_async_remote_copy(
        src_ref=mixed.at[1 - role],
        dst_ref=mixed_in,
        send_sem=mix_sem.at[0],
        recv_sem=mix_sem.at[1],
        device_id={"ctx": partner},
        device_id_type=MESH,
    )

    @pl.loop(0, micro * pairs, unroll=4)
    def _(u):
        mix((1 - role) * (micro * pairs) + u)

    send_mixed.start()

    @pl.loop(0, micro * pairs, unroll=4)
    def _(u):
        mix(role * (micro * pairs) + u)

    send_mixed.wait_recv()

    pltpu.make_async_remote_copy(
        src_ref=full_b.at[pl.ds(0, (total - 1) * depth_b)],
        dst_ref=full_b.at[pl.ds(0, (total - 1) * depth_b)],
        send_sem=hand_sem.at[0],
        recv_sem=whole_sem.at[0],
        device_id={"section": lax.rem(section + sections - 1, sections)},
        device_id_type=MESH,
    ).wait_recv()

    here = pl.ds(pl.multiple_of(role * half_inner, TILE), half_inner)
    there = pl.ds(pl.multiple_of((1 - role) * half_inner, TILE), half_inner)

    @pl.loop(0, stripes)
    def _(c):
        for piece in range(stripe // 256):
            cols = pl.ds(pl.multiple_of(c * stripe + piece * 256, 256), 256)
            product = dot(mixed[role], full_b[here, cols]) + dot(mixed_in[...], full_b[there, cols])
            for m in range(micro):
                result[m, :, cols] = (
                    xbuf[role, m, :, cols].astype(f32) + product[m * rows : (m + 1) * rows]
                ).astype(bf16)

        put(c).start()

        @pl.when(section < sections - 1)
        def _():
            for to in (1, 0):
                pass_on(to, c).start()

    @pl.when(section == 0)
    def _():
        pl.semaphore_wait(start_sem, 1)
        relay_own()
        receive(1, 1, farthest)
        drain(0)
        drain(1)
        for c in range(stripes):
            send_x(c).wait_send()

    hand.wait_send()
    send_decay.wait_send()
    send_mixed.wait_send()

    @pl.loop(1, peers)
    def _(k):
        peer = lax.rem(my_peer + k, peers)
        first(peer, my_peer).wait_send()
        second(peer, my_peer).wait_send()

    for c in range(stripes):
        put(c).wait()

    @pl.when(section < sections - 1)
    def _():
        for c in range(stripes):
            for to in range(2):
                pass_on(to, c).wait_send()


def shards(sizes, sections, tokens, qkv_weight, out_weight, log_decay):
    micro, rows, width = tokens.shape
    total = int(np.prod(sizes))
    peers = total // 2
    heads = log_decay.shape[3]
    own = (qkv_weight[0], out_weight[0])
    inner = own[1].shape[0] * total
    half = inner // 2
    lanes = 2 * inner // heads
    part = micro * inner // 2 // total
    plan = [pieces(s.shape[0], sizes, n) for s, n in zip(own, (2, 2))]
    count = 2 * len(plan[0]) + len(plan[1])
    stripes = max(1, width // 512)
    f32, bf16 = jnp.float32, jnp.bfloat16
    dma = pltpu.SemaphoreType.DMA
    anywhere = pl.BlockSpec(memory_space=pl.ANY)
    vmem = pl.BlockSpec(memory_space=pltpu.VMEM)
    result = pl.pallas_call(
        functools.partial(whole_kernel, sizes, sections, plan, heads),
        out_shape=jax.ShapeDtypeStruct(tokens.shape, tokens.dtype),
        in_specs=[anywhere, vmem, anywhere, anywhere],
        out_specs=anywhere,
        scratch_shapes=[
            pltpu.VMEM((2, width, 3 * half), bf16),
            pltpu.VMEM((inner, width), bf16),
            pltpu.VMEM((inner, width), bf16),
            pltpu.VMEM((2, micro, rows, width), bf16),
            pltpu.VMEM((2 * micro, rows, lanes), f32),
            pltpu.VMEM((2, micro * rows, 3 * half), bf16),
            pltpu.VMEM((micro, heads, rows), f32),
            pltpu.VMEM((2 * micro, rows, heads // 2 * lanes), f32),
            pltpu.VMEM((2 * micro, heads // 2, rows), f32),
            pltpu.VMEM((2, micro * rows, half), f32),
            pltpu.VMEM((2, micro * rows, half), bf16),
            pltpu.VMEM((micro * rows, half), bf16),
            pltpu.VMEM((micro, rows, width), bf16),
            pltpu.VMEM((peers, 2, part + TILE, lanes), bf16),
            pltpu.VMEM((peers, 2, part + TILE, lanes), bf16),
            pltpu.VMEM((peers, 2, part, lanes), bf16),
            pltpu.VMEM((peers, 2, part, lanes), bf16),
            dma((total, count)),
            dma((total, count)),
            dma((8,)),
            dma((3, stripes)),
            dma((2, stripes)),
            dma((stripes,)),
            dma((2,)),
            dma((2,)),
            dma((2,)),
            dma((1,)),
            pltpu.SemaphoreType.REGULAR,
            dma((peers,)),
            dma((peers,)),
            dma((peers,)),
            dma((peers,)),
        ],
        compiler_params=pltpu.CompilerParams(
            collective_id=0, has_side_effects=True, vmem_limit_bytes=60 * 2**20
        ),
        name="mixer_stack",
    )(tokens, jnp.swapaxes(log_decay[0], 1, 2), *own)
    return result[None]


def solution(mesh):
    in_specs = (
        P(None, "ctx", None),
        P("section", "ctx", None),
        P("section", "ctx", None),
        P("section", None, "ctx", None),
    )
    out_specs = P("section", None, "ctx", None)
    return jax.shard_map(
        functools.partial(shards, line_sizes(mesh), mesh.shape["section"]),
        mesh=mesh,
        in_specs=in_specs,
        out_specs=out_specs,
        check_vma=False,
    )
```

```python
import functools

import jax
import jax.numpy as jnp
import numpy as np
from jax import lax
from jax.experimental import pallas as pl
from jax.experimental.pallas import tpu as pltpu
from jax.sharding import PartitionSpec as P

MESH = pl.DeviceIdType.MESH
TILE = 16


def line_sizes(mesh):
    total = mesh.shape["ctx"]
    places = np.moveaxis(mesh.devices, mesh.axis_names.index("ctx"), 0).reshape(total, -1)[:, 0]
    sizes, left = [], total
    try:
        coords = [tuple(d.coords) for d in places]
    except AttributeError:
        coords = None
    if coords is not None:
        step = 1
        while step < total:
            changed = [a != b for a, b in zip(coords[0], coords[step])]
            axis = changed.index(True)
            size = 1
            while step * size < total and (
                size == 1 or (coords[step * size][axis] != coords[0][axis]
                and all(coords[step * size][i] == coords[0][i] for i in range(3) if i != axis))
            ):
                size += 1
            while total % (step * size):
                size -= 1
            sizes.insert(0, size)
            step *= size
    else:
        while left > 1:
            sizes.append(2)
            left //= 2
    return tuple(sizes)


def pair_axis(sizes):
    return next(i for i, s in enumerate(sizes) if s % 2 == 0)


def pieces(rows, sizes, parts):
    d, axis = len(sizes), pair_axis(sizes)
    rest = tuple(i for i in range(d) if i != axis)
    orders = [(axis,) + rest[::-1], (axis,) + rest]
    units = rows // TILE
    parts = min(parts, units)
    cuts = [units * p // parts * TILE for p in range(parts)] + [rows]
    return [(orders[p % 2], cuts[p], cuts[p + 1] - cuts[p]) for p in range(parts)]


def place_in_line(me, size, t):
    low = jnp.minimum(me, size - 1 - me)
    half = lax.div(t + 1, 2)
    near = jnp.where(lax.rem(t, 2) == 1, me + half, me - half)
    far = jnp.where(me < size - 1 - me, me + (t - low), me - (t - low))
    return jnp.where(t <= 2 * low, near, far)


def dot(a, b, contract=((1,), (0,)), precision=None):
    return lax.dot_general(
        a, b, (contract, ((), ())), precision=precision, preferred_element_type=jnp.float32
    )


def whole_kernel(
    sizes, sections, plan, heads, tokens, decay, shard_a, shard_b, out,
    full_a, full_b, relay_b, xbuf, scales, proj, decays, cumx, cumt, intra, mixed, mixed_in, result,
    items, got, carried, landed,
    send_sem, recv_sem, own_sem, x_send, x_recv, put_sem, d_sem, mix_sem, hand_sem, whole_sem, start_sem, s1, r1, s2, r2,
):
    f32, bf16 = jnp.float32, jnp.bfloat16
    both = jnp.logical_and
    d = len(sizes)
    axis = pair_axis(sizes)
    total = int(np.prod(sizes))
    strides = [int(np.prod(sizes[i + 1 :])) for i in range(d)]
    me = lax.axis_index("ctx")
    section = lax.axis_index("section")

    def coords_of(index):
        return [lax.rem(lax.div(index, strides[i]), sizes[i]) for i in range(d)]

    mine = coords_of(me)
    role = lax.rem(mine[axis], 2)
    partner = me + (1 - 2 * role) * strides[axis]
    peers = total // 2
    wide = strides[axis] * sizes[axis]

    def peer_of(index):
        line = lax.rem(lax.div(index, strides[axis]), sizes[axis])
        return (
            lax.div(index, wide) * (wide // 2)
            + lax.div(line, 2) * strides[axis]
            + lax.rem(index, strides[axis])
        )

    def device_of(peer, side):
        line = lax.rem(lax.div(peer, strides[axis]), sizes[axis] // 2)
        return (
            lax.div(peer, wide // 2) * wide
            + (2 * line + side) * strides[axis]
            + lax.rem(peer, strides[axis])
        )

    my_peer = peer_of(me)

    ways = [(i, sign) for i in range(d) for sign in (1, -1)]
    most_ways = sum(min(n - 1, 2) for n in sizes)
    _, micro, rows, width = xbuf.shape
    half_inner = mixed.shape[2]
    half_heads = heads // 2
    head_dim = half_inner // half_heads
    pairs = half_heads // 2
    lanes = 2 * head_dim
    part = carried.shape[2]
    stripes = x_recv.shape[1]
    stripe = width // stripes
    depth_a, depth_b = shard_a.shape[0], shard_b.shape[0]

    staged_a = []
    for h in range(2):
        for which in range(3):
            staged_a.append(
                pltpu.make_async_copy(
                    shard_a.at[:, pl.ds((2 * which + h) * half_inner, half_inner)],
                    full_a.at[
                        h, pl.ds(pl.multiple_of(me * depth_a, TILE), depth_a),
                        pl.ds(which * half_inner, half_inner),
                    ],
                    own_sem.at[2 + 3 * h + which],
                )
            )
    staged_b = pltpu.make_async_copy(
        shard_b, full_b.at[pl.ds(pl.multiple_of(me * depth_b, TILE), depth_b)], own_sem.at[0]
    )
    x_own = pltpu.make_async_copy(tokens, xbuf.at[role], own_sem.at[1])
    for c in staged_a:
        c.start()
    staged_b.start()

    @pl.when(section == 0)
    def _():
        x_own.start()

    barrier = pltpu.get_barrier_semaphore()

    @pl.loop(1, peers)
    def _(k):
        pl.semaphore_signal(
            barrier, inc=1,
            device_id={"ctx": device_of(lax.rem(my_peer + k, peers), role)}, device_id_type=MESH,
        )

    met = jnp.int32(0)
    for sign in (1, -1):
        there = both(mine[axis] + sign >= 0, mine[axis] + sign < sizes[axis])
        met = met + there.astype(jnp.int32)

        @pl.when(there)
        def _(sign=sign):
            pl.semaphore_signal(
                barrier, inc=1, device_id={"ctx": me + sign * strides[axis]}, device_id_type=MESH
            )

    sides = [1] if sections == 2 else [1, sections - 1]
    for away in sides:
        for chip in (me, partner):
            pl.semaphore_signal(
                barrier, inc=1,
                device_id={"section": lax.rem(section + away, sections), "ctx": chip},
                device_id_type=MESH,
            )

    pl.semaphore_wait(barrier, 2 * len(sides) + (peers - 1) + met)

    parts = [(0, h) + p for h in range(2) for p in plan[0]] + [(1, None) + p for p in plan[1]]

    def block(index, begin, size):
        a, h = parts[index][:2]
        return full_a.at[h, pl.ds(begin, size)] if a == 0 else relay_b.at[pl.ds(begin, size)]

    def copy(source, index, way):
        a, _, _, at, size = parts[index]
        i, sign = way
        target = block(
            index, pl.multiple_of(source * (depth_a, depth_b)[a] + at, TILE), size
        )
        return pltpu.make_async_remote_copy(
            src_ref=target,
            dst_ref=target,
            send_sem=send_sem.at[source, index],
            recv_sem=recv_sem.at[source, index],
            device_id={"ctx": me + sign * strides[i]},
            device_id_type=MESH,
        )

    def sent(source, index, times):
        target = block(index, 0, times * parts[index][4])
        return pltpu.make_async_remote_copy(
            src_ref=target,
            dst_ref=target,
            send_sem=send_sem.at[source, index],
            recv_sem=recv_sem.at[source, index],
            device_id={"ctx": partner},
            device_id_type=MESH,
        )

    def deliver(source, index):
        _, _, _, at, size = parts[index]
        span = pl.ds(pl.multiple_of(source * depth_b + at, TILE), size)
        return pltpu.make_async_remote_copy(
            src_ref=relay_b.at[span],
            dst_ref=full_b.at[span],
            send_sem=send_sem.at[source, index],
            recv_sem=whole_sem.at[0],
            device_id={"section": lax.rem(section + sections - 1, sections)},
            device_id_type=MESH,
        )

    def inside(i, place):
        return both(place >= 0, place < sizes[i])

    def goes(coords, index, way):
        h, order = parts[index][1:3]
        i, sign = way
        ok = both(inside(i, mine[i] + sign), (mine[i] - coords[i]) * sign >= 0)
        for later in order[order.index(i) + 1 :]:
            ok = both(ok, mine[later] == coords[later])
        if h is not None:
            if i == axis:
                ok = both(ok, jnp.logical_or(role != h, inside(i, mine[i] + 2 * sign)))
            else:
                ok = both(ok, role == h)
        return ok

    def onward(source, coords, index):
        for way in ways:
            @pl.when(goes(coords, index, way))
            def _(way=way):
                copy(source, index, way).start()

    def arrives(coords, index):
        h = parts[index][1]
        if h is None:
            return None
        gap = mine[axis] - coords[axis]
        beyond = jnp.where(gap > 0, inside(axis, mine[axis] + 1), inside(axis, mine[axis] - 1))
        ok = both(gap != 0, beyond)
        for i in range(d):
            if i != axis:
                ok = both(ok, mine[i] == coords[i])
        return jnp.logical_or(role == h, ok)

    def of(wanted):
        return [index for index in range(len(parts)) if parts[index][0] == wanted]

    def source_of(j):
        coords = coords_of(j)
        for i in range(d):
            if i == axis:
                coords[i] = place_in_line(mine[i], sizes[i], sizes[i] - 1 - coords[i])
            else:
                coords[i] = lax.rem(mine[i] + coords[i], sizes[i])
        return sum(c * s for c, s in zip(coords, strides)), coords

    def receive(wanted, least, most):
        @pl.loop(least * total, most * total)
        def _(k):
            hops, j = lax.div(k, total), lax.rem(k, total)
            source, coords = source_of(j)
            away = sum(jnp.abs(mine[i] - coords[i]) for i in range(d))

            @pl.when(away == hops)
            def _():
                for index in of(wanted):
                    def take(index=index):
                        copy(source, index, ways[0]).wait_recv()
                        onward(source, coords, index)
                        if wanted == 1:
                            deliver(source, index).start()

                    ok = arrives(coords, index)
                    if ok is None:
                        take()
                    else:
                        pl.when(ok)(take)

    def drain(wanted):
        @pl.loop(0, total)
        def _(source):
            coords = coords_of(source)
            for index in of(wanted):
                times = sum(goes(coords, index, way).astype(jnp.int32) for way in ways)
                ok = arrives(coords, index)
                if ok is not None:
                    times = jnp.where(jnp.logical_or(source == me, ok), times, 0)
                if wanted == 1:
                    times = times + (source != me).astype(jnp.int32)
                for n in range(1, most_ways + 1 + wanted):
                    @pl.when(times == n)
                    def _(index=index, n=n):
                        sent(source, index, n).wait_send()

    farthest = sum(n - 1 for n in sizes) + 1

    def columns(c):
        return pl.ds(pl.multiple_of(c * stripe, stripe), stripe)

    def send_x(c):
        return pltpu.make_async_remote_copy(
            src_ref=xbuf.at[role, :, :, columns(c)],
            dst_ref=xbuf.at[role, :, :, columns(c)],
            send_sem=x_send.at[2, c],
            recv_sem=x_recv.at[1, c],
            device_id={"ctx": partner},
            device_id_type=MESH,
        )

    def pass_on(to, c):
        return pltpu.make_async_remote_copy(
            src_ref=result.at[:, :, columns(c)],
            dst_ref=xbuf.at[role, :, :, columns(c)],
            send_sem=x_send.at[to, c],
            recv_sem=x_recv.at[to, c],
            device_id={"section": lax.rem(section + 1, sections), "ctx": (me, partner)[to]},
            device_id_type=MESH,
        )

    def wait_x(which, c):
        place = role if which == 0 else 1 - role
        pltpu.make_async_remote_copy(
            src_ref=result.at[:, :, columns(c)],
            dst_ref=xbuf.at[place, :, :, columns(c)],
            send_sem=x_send.at[which, c],
            recv_sem=x_recv.at[which, c],
            device_id={"ctx": partner},
            device_id_type=MESH,
        ).wait_recv()

    def put(c):
        return pltpu.make_async_copy(
            result.at[:, :, columns(c)], out.at[:, :, columns(c)], put_sem.at[c]
        )

    hand = pltpu.make_async_remote_copy(
        src_ref=shard_b,
        dst_ref=relay_b.at[pl.ds(pl.multiple_of(me * depth_b, TILE), depth_b)],
        send_sem=hand_sem.at[0],
        recv_sem=hand_sem.at[1],
        device_id={"section": lax.rem(section + 1, sections)},
        device_id_type=MESH,
    )
    send_decay = pltpu.make_async_remote_copy(
        src_ref=decay,
        dst_ref=decays,
        send_sem=d_sem.at[0],
        recv_sem=d_sem.at[1],
        device_id={"ctx": partner},
        device_id_type=MESH,
    )
    send_decay.start()
    hand.start()
    for c in staged_a:
        c.wait()

    @pl.when(section == 0)
    def _():
        for index in of(0):
            onward(me, mine, index)
        x_own.wait()

    staged_b.wait()

    at_row = lax.broadcasted_iota(jnp.int32, (rows, rows), 0)
    at_col = lax.broadcasted_iota(jnp.int32, (rows, rows), 1)
    causal = at_row >= at_col
    upper = (at_row <= at_col).astype(f32)

    def accumulate(place, source):
        spread = (
            lax.broadcasted_iota(jnp.int32, (half_heads, half_heads * lanes), 0)
            == lax.broadcasted_iota(jnp.int32, (half_heads, half_heads * lanes), 1) // lanes
        ).astype(f32)
        for m in range(micro):
            own = source[m, pl.ds(pl.multiple_of(role * half_heads, half_heads), half_heads), :]
            summed = dot(own, upper, precision=lax.Precision.HIGHEST)
            cumt[place * micro + m] = summed
            cumx[place * micro + m] = dot(
                summed, spread, ((0,), (0,)), precision=lax.Precision.HIGHEST
            )

    accumulate(role, decay)
    send_decay.wait_recv()
    accumulate(1 - role, decays)

    def let_next_start():
        pl.semaphore_signal(
            start_sem, inc=1, device_id={"section": lax.rem(section + 1, sections)},
            device_id_type=MESH,
        )

    def measure_rows(place, m):
        @pl.loop(0, rows // TILE, unroll=4)
        def _(q):
            at = pl.multiple_of(q * TILE, TILE)
            wide_rows = xbuf[place, m, pl.ds(at, TILE), :].astype(f32)
            scale = lax.rsqrt(jnp.mean(wide_rows * wide_rows, axis=-1, keepdims=True) + 1e-05)
            scales[place * micro + m, pl.ds(at, TILE), :] = jnp.broadcast_to(scale, (TILE, lanes))

    def relay_own():
        hand.wait_recv()
        for index in of(1):
            onward(me, mine, index)

    def send_stripes(least, most):
        @pl.when(section == 0)
        def _():
            for c in range(least, most):
                send_x(c).start()

    @pl.when(section > 0)
    def _():
        pl.semaphore_wait(start_sem, 1)
        relay_own()
        receive(1, 1, 3)
        for index in of(0):
            onward(me, mine, index)
        receive(1, 3, 4)
        receive(0, 1, 2)
        receive(1, 4, 5)
        receive(0, 2, 3)
        let_next_start()
        receive(1, 5, farthest)
        receive(0, 3, farthest - 1)
        for c in range(stripes):
            wait_x(0, c)
        for m in range(micro):
            measure_rows(role, m)
        for c in range(stripes):
            wait_x(1, c)
        for m in range(micro):
            measure_rows(1 - role, m)
        receive(0, farthest - 1, farthest)

    @pl.when(section == 0)
    def _():
        receive(0, 1, 2)
        send_stripes(stripes * 0 // 4, stripes * 2 // 4)
        receive(0, 2, 3)
        send_stripes(stripes * 2 // 4, stripes * 3 // 4)
        receive(0, 3, 4)
        send_stripes(stripes * 3 // 4, stripes * 4 // 4)
        let_next_start()
        for m in range(micro):
            measure_rows(role, m)
        receive(0, 4, farthest - 1)
        for c in range(stripes):
            wait_x(1, c)
        for m in range(micro):
            measure_rows(1 - role, m)
        receive(0, farthest - 1, farthest)

    def project(place):
        @pl.loop(0, 3 * half_inner // 512)
        def _(c):
            cols = pl.ds(pl.multiple_of(c * 512, 512), 512)
            inputs = xbuf[place].reshape(micro * rows, width)
            product = dot(inputs, full_a[role, :, cols])
            scale = jnp.concatenate(
                [scales[place * micro + m] for m in range(micro)], axis=0
            )
            scale = jnp.concatenate([scale] * (512 // lanes), axis=1)
            proj[place, :, cols] = (product * scale).astype(bf16)

    project(role)
    project(1 - role)

    first_half = lax.broadcasted_iota(jnp.int32, (rows, lanes), 1) < head_dim
    first_item = lax.broadcasted_iota(jnp.int32, (head_dim, lanes), 1) < head_dim
    per_pair = head_dim // part

    def located(u):
        g, p = lax.div(u, pairs), lax.rem(u, pairs)
        place, m = lax.div(g, micro), lax.rem(g, micro)
        span = pl.ds(pl.multiple_of(m * rows, TILE), rows)

        def column(which):
            return pl.ds(pl.multiple_of(which * half_inner + p * lanes, lanes), lanes)

        def cum(h):
            return cumx[g, :, pl.ds(pl.multiple_of((2 * p + h) * lanes, lanes), lanes)]

        return place, m, p, span, column, cum

    @pl.loop(0, 2 * micro * pairs, unroll=4)
    def _(u):
        place, m, p, span, column, cum = located(u)
        decayed = jnp.where(first_half, cum(0), cum(1))
        ending = decayed[rows - 1 :, :]
        scaled = (proj[place, span, column(1)].astype(f32) * jnp.exp(ending - decayed)).astype(bf16)
        state = dot(scaled, proj[place, span, column(2)], ((0,), (0,)))
        packed = jnp.where(first_item, state[:head_dim], state[head_dim:]).astype(bf16)
        weight = jnp.broadcast_to(jnp.exp(ending), (TILE, lanes)).astype(bf16)
        for piece in range(per_pair):
            to = (m * pairs + p) * per_pair + piece
            items[to, place, :part, :] = packed[piece * part : (piece + 1) * part]
            items[to, place, part:, :] = weight

    def first(to, slot_from):
        return pltpu.make_async_remote_copy(
            src_ref=items.at[to],
            dst_ref=got.at[slot_from],
            send_sem=s1.at[to],
            recv_sem=r1.at[slot_from],
            device_id={"ctx": device_of(to, role)},
            device_id_type=MESH,
        )

    def second(to, slot_from):
        return pltpu.make_async_remote_copy(
            src_ref=carried.at[to],
            dst_ref=landed.at[slot_from],
            send_sem=s2.at[to],
            recv_sem=r2.at[slot_from],
            device_id={"ctx": device_of(to, role)},
            device_id_type=MESH,
        )

    @pl.loop(1, peers)
    def _(k):
        first(lax.rem(my_peer + k, peers), my_peer).start()

    got[my_peer] = items[my_peer]

    def within(u):
        place, m, p, span, column, cum = located(u)
        queries, keys, values = (proj[place, span, column(i)] for i in range(3))
        outs = []
        for h in range(2):
            own_half = first_half if h == 0 else jnp.logical_not(first_half)
            scores = dot(jnp.where(own_half, queries, jnp.zeros_like(queries)), keys, ((1,), (1,)))
            gap = cum(h) - cumt[place * micro + m, pl.ds(2 * p + h, 1), :]
            weights = jnp.where(
                causal, scores * jnp.exp(jnp.where(causal, gap, 0.0)), 0.0
            ).astype(bf16)
            outs.append(dot(weights, values))
        intra[place, span, column(0)] = jnp.where(first_half, outs[0], outs[1])

    @pl.loop(0, micro * pairs, unroll=4)
    def _(u):
        within((1 - role) * (micro * pairs) + u)

    def step(b, acc):
        peer = peer_of(b)
        side = lax.rem(lax.rem(lax.div(b, strides[axis]), sizes[axis]), 2)

        @pl.when(both(peer != my_peer, side == 0))
        def _():
            first(peer, peer).wait_recv()

        low = acc.astype(bf16)
        carried[peer, side] = low

        @pl.when(both(peer != my_peer, side == 1))
        def _():
            second(peer, my_peer).start()

        @pl.when(peer == my_peer)
        def _():
            landed[my_peer, side] = low

        item = got[peer, side].astype(f32)
        return acc * item[part : part + 1] + item[:part]

    @pl.when(section > 0)
    def _():
        drain(0)

    lax.fori_loop(0, total, step, jnp.zeros((part, lanes), f32))

    @pl.loop(0, micro * pairs, unroll=4)
    def _(u):
        within(role * (micro * pairs) + u)

    @pl.when(section > 0)
    def _():
        drain(1)

    @pl.loop(1, peers)
    def _(k):
        peer = lax.rem(my_peer + k, peers)
        second(peer, peer).wait_recv()

    def mix(u):
        place, m, p, span, column, cum = located(u)
        low = jnp.concatenate(
            [landed[(m * pairs + p) * per_pair + i, place] for i in range(per_pair)], axis=0
        )
        none = jnp.zeros_like(low)
        block = jnp.concatenate(
            [jnp.where(first_item, low, none), jnp.where(first_item, none, low)], axis=0
        )
        decayed = jnp.where(first_half, cum(0), cum(1))
        mixture = (
            intra[place, span, column(0)]
            + dot(proj[place, span, column(0)], block) * jnp.exp(decayed)
        )
        squares = mixture * mixture
        factors = [
            lax.rsqrt(
                jnp.sum(jnp.where(own, squares, 0.0), axis=-1, keepdims=True) / head_dim + 1e-05
            )
            for own in (first_half, jnp.logical_not(first_half))
        ]
        mixed[place, span, column(0)] = (
            mixture * jnp.where(first_half, factors[0], factors[1])
        ).astype(bf16)

    send_mixed = pltpu.make_async_remote_copy(
        src_ref=mixed.at[1 - role],
        dst_ref=mixed_in,
        send_sem=mix_sem.at[0],
        recv_sem=mix_sem.at[1],
        device_id={"ctx": partner},
        device_id_type=MESH,
    )

    @pl.loop(0, micro * pairs, unroll=4)
    def _(u):
        mix((1 - role) * (micro * pairs) + u)

    send_mixed.start()

    @pl.loop(0, micro * pairs, unroll=4)
    def _(u):
        mix(role * (micro * pairs) + u)

    send_mixed.wait_recv()

    pltpu.make_async_remote_copy(
        src_ref=full_b.at[pl.ds(0, (total - 1) * depth_b)],
        dst_ref=full_b.at[pl.ds(0, (total - 1) * depth_b)],
        send_sem=hand_sem.at[0],
        recv_sem=whole_sem.at[0],
        device_id={"section": lax.rem(section + sections - 1, sections)},
        device_id_type=MESH,
    ).wait_recv()

    here = pl.ds(pl.multiple_of(role * half_inner, TILE), half_inner)
    there = pl.ds(pl.multiple_of((1 - role) * half_inner, TILE), half_inner)

    @pl.loop(0, stripes)
    def _(c):
        for piece in range(stripe // 256):
            cols = pl.ds(pl.multiple_of(c * stripe + piece * 256, 256), 256)
            product = dot(mixed[role], full_b[here, cols]) + dot(mixed_in[...], full_b[there, cols])
            for m in range(micro):
                result[m, :, cols] = (
                    xbuf[role, m, :, cols].astype(f32) + product[m * rows : (m + 1) * rows]
                ).astype(bf16)

        put(c).start()

        @pl.when(section < sections - 1)
        def _():
            for to in (1, 0):
                pass_on(to, c).start()

    @pl.when(section == 0)
    def _():
        pl.semaphore_wait(start_sem, 1)
        relay_own()
        receive(1, 1, farthest)
        drain(0)
        drain(1)
        for c in range(stripes):
            send_x(c).wait_send()

    hand.wait_send()
    send_decay.wait_send()
    send_mixed.wait_send()

    @pl.loop(1, peers)
    def _(k):
        peer = lax.rem(my_peer + k, peers)
        first(peer, my_peer).wait_send()
        second(peer, my_peer).wait_send()

    for c in range(stripes):
        put(c).wait()

    @pl.when(section < sections - 1)
    def _():
        for c in range(stripes):
            for to in range(2):
                pass_on(to, c).wait_send()


def shards(sizes, sections, tokens, qkv_weight, out_weight, log_decay):
    micro, rows, width = tokens.shape
    total = int(np.prod(sizes))
    peers = total // 2
    heads = log_decay.shape[3]
    own = (qkv_weight[0], out_weight[0])
    inner = own[1].shape[0] * total
    half = inner // 2
    lanes = 2 * inner // heads
    part = micro * inner // 2 // total
    plan = [pieces(s.shape[0], sizes, n) for s, n in zip(own, (2, 4))]
    count = 2 * len(plan[0]) + len(plan[1])
    stripes = max(1, width // 512)
    f32, bf16 = jnp.float32, jnp.bfloat16
    dma = pltpu.SemaphoreType.DMA
    anywhere = pl.BlockSpec(memory_space=pl.ANY)
    vmem = pl.BlockSpec(memory_space=pltpu.VMEM)
    result = pl.pallas_call(
        functools.partial(whole_kernel, sizes, sections, plan, heads),
        out_shape=jax.ShapeDtypeStruct(tokens.shape, tokens.dtype),
        in_specs=[anywhere, vmem, anywhere, anywhere],
        out_specs=anywhere,
        scratch_shapes=[
            pltpu.VMEM((2, width, 3 * half), bf16),
            pltpu.VMEM((inner, width), bf16),
            pltpu.VMEM((inner, width), bf16),
            pltpu.VMEM((2, micro, rows, width), bf16),
            pltpu.VMEM((2 * micro, rows, lanes), f32),
            pltpu.VMEM((2, micro * rows, 3 * half), bf16),
            pltpu.VMEM((micro, heads, rows), f32),
            pltpu.VMEM((2 * micro, rows, heads // 2 * lanes), f32),
            pltpu.VMEM((2 * micro, heads // 2, rows), f32),
            pltpu.VMEM((2, micro * rows, half), f32),
            pltpu.VMEM((2, micro * rows, half), bf16),
            pltpu.VMEM((micro * rows, half), bf16),
            pltpu.VMEM((micro, rows, width), bf16),
            pltpu.VMEM((peers, 2, part + TILE, lanes), bf16),
            pltpu.VMEM((peers, 2, part + TILE, lanes), bf16),
            pltpu.VMEM((peers, 2, part, lanes), bf16),
            pltpu.VMEM((peers, 2, part, lanes), bf16),
            dma((total, count)),
            dma((total, count)),
            dma((8,)),
            dma((3, stripes)),
            dma((2, stripes)),
            dma((stripes,)),
            dma((2,)),
            dma((2,)),
            dma((2,)),
            dma((1,)),
            pltpu.SemaphoreType.REGULAR,
            dma((peers,)),
            dma((peers,)),
            dma((peers,)),
            dma((peers,)),
        ],
        compiler_params=pltpu.CompilerParams(
            collective_id=0, has_side_effects=True, vmem_limit_bytes=60 * 2**20
        ),
        name="mixer_stack",
    )(tokens, jnp.swapaxes(log_decay[0], 1, 2), *own)
    return result[None]


def solution(mesh):
    in_specs = (
        P(None, "ctx", None),
        P("section", "ctx", None),
        P("section", "ctx", None),
        P("section", None, "ctx", None),
    )
    out_specs = P("section", None, "ctx", None)
    return jax.shard_map(
        functools.partial(shards, line_sizes(mesh), mesh.shape["section"]),
        mesh=mesh,
        in_specs=in_specs,
        out_specs=out_specs,
        check_vma=False,
    )
```

```python
import functools

import jax
import jax.numpy as jnp
import numpy as np
from jax import lax
from jax.experimental import pallas as pl
from jax.experimental.pallas import tpu as pltpu
from jax.sharding import PartitionSpec as P

MESH = pl.DeviceIdType.MESH
TILE = 16


def line_sizes(mesh):
    total = mesh.shape["ctx"]
    places = np.moveaxis(mesh.devices, mesh.axis_names.index("ctx"), 0).reshape(total, -1)[:, 0]
    sizes, left = [], total
    try:
        coords = [tuple(d.coords) for d in places]
    except AttributeError:
        coords = None
    if coords is not None:
        step = 1
        while step < total:
            changed = [a != b for a, b in zip(coords[0], coords[step])]
            axis = changed.index(True)
            size = 1
            while step * size < total and (
                size == 1 or (coords[step * size][axis] != coords[0][axis]
                and all(coords[step * size][i] == coords[0][i] for i in range(3) if i != axis))
            ):
                size += 1
            while total % (step * size):
                size -= 1
            sizes.insert(0, size)
            step *= size
    else:
        while left > 1:
            sizes.append(2)
            left //= 2
    return tuple(sizes)


def pair_axis(sizes):
    return next(i for i, s in enumerate(sizes) if s % 2 == 0)


def pieces(rows, sizes, parts):
    d, axis = len(sizes), pair_axis(sizes)
    rest = tuple(i for i in range(d) if i != axis)
    orders = [(axis,) + rest[::-1], (axis,) + rest]
    units = rows // TILE
    parts = min(parts, units)
    cuts = [units * p // parts * TILE for p in range(parts)] + [rows]
    return [(orders[p % 2], cuts[p], cuts[p + 1] - cuts[p]) for p in range(parts)]


def place_in_line(me, size, t):
    low = jnp.minimum(me, size - 1 - me)
    half = lax.div(t + 1, 2)
    near = jnp.where(lax.rem(t, 2) == 1, me + half, me - half)
    far = jnp.where(me < size - 1 - me, me + (t - low), me - (t - low))
    return jnp.where(t <= 2 * low, near, far)


def dot(a, b, contract=((1,), (0,)), precision=None):
    return lax.dot_general(
        a, b, (contract, ((), ())), precision=precision, preferred_element_type=jnp.float32
    )


def whole_kernel(
    sizes, sections, plan, heads, tokens, decay, shard_a, shard_b, out,
    full_a, full_b, relay_b, xbuf, scales, proj, decays, cumx, cumt, intra, mixed, mixed_in, result,
    items, got, carried, landed,
    send_sem, recv_sem, own_sem, x_send, x_recv, put_sem, d_sem, mix_sem, hand_sem, whole_sem, start_sem, s1, r1, s2, r2,
):
    f32, bf16 = jnp.float32, jnp.bfloat16
    both = jnp.logical_and
    d = len(sizes)
    axis = pair_axis(sizes)
    total = int(np.prod(sizes))
    strides = [int(np.prod(sizes[i + 1 :])) for i in range(d)]
    me = lax.axis_index("ctx")
    section = lax.axis_index("section")

    def coords_of(index):
        return [lax.rem(lax.div(index, strides[i]), sizes[i]) for i in range(d)]

    mine = coords_of(me)
    role = lax.rem(mine[axis], 2)
    partner = me + (1 - 2 * role) * strides[axis]
    peers = total // 2
    wide = strides[axis] * sizes[axis]

    def peer_of(index):
        line = lax.rem(lax.div(index, strides[axis]), sizes[axis])
        return (
            lax.div(index, wide) * (wide // 2)
            + lax.div(line, 2) * strides[axis]
            + lax.rem(index, strides[axis])
        )

    def device_of(peer, side):
        line = lax.rem(lax.div(peer, strides[axis]), sizes[axis] // 2)
        return (
            lax.div(peer, wide // 2) * wide
            + (2 * line + side) * strides[axis]
            + lax.rem(peer, strides[axis])
        )

    my_peer = peer_of(me)

    ways = [(i, sign) for i in range(d) for sign in (1, -1)]
    most_ways = sum(min(n - 1, 2) for n in sizes)
    _, micro, rows, width = xbuf.shape
    half_inner = mixed.shape[2]
    half_heads = heads // 2
    head_dim = half_inner // half_heads
    pairs = half_heads // 2
    lanes = 2 * head_dim
    part = carried.shape[2]
    stripes = x_recv.shape[1]
    stripe = width // stripes
    depth_a, depth_b = shard_a.shape[0], shard_b.shape[0]

    staged_a = []
    for h in range(2):
        for which in range(3):
            staged_a.append(
                pltpu.make_async_copy(
                    shard_a.at[:, pl.ds((2 * which + h) * half_inner, half_inner)],
                    full_a.at[
                        h, pl.ds(pl.multiple_of(me * depth_a, TILE), depth_a),
                        pl.ds(which * half_inner, half_inner),
                    ],
                    own_sem.at[2 + 3 * h + which],
                )
            )
    staged_b = pltpu.make_async_copy(
        shard_b, full_b.at[pl.ds(pl.multiple_of(me * depth_b, TILE), depth_b)], own_sem.at[0]
    )
    x_own = pltpu.make_async_copy(tokens, xbuf.at[role], own_sem.at[1])
    for c in staged_a:
        c.start()
    staged_b.start()

    @pl.when(section == 0)
    def _():
        x_own.start()

    barrier = pltpu.get_barrier_semaphore()

    @pl.loop(1, peers)
    def _(k):
        pl.semaphore_signal(
            barrier, inc=1,
            device_id={"ctx": device_of(lax.rem(my_peer + k, peers), role)}, device_id_type=MESH,
        )

    met = jnp.int32(0)
    for sign in (1, -1):
        there = both(mine[axis] + sign >= 0, mine[axis] + sign < sizes[axis])
        met = met + there.astype(jnp.int32)

        @pl.when(there)
        def _(sign=sign):
            pl.semaphore_signal(
                barrier, inc=1, device_id={"ctx": me + sign * strides[axis]}, device_id_type=MESH
            )

    sides = [1] if sections == 2 else [1, sections - 1]
    for away in sides:
        for chip in (me, partner):
            pl.semaphore_signal(
                barrier, inc=1,
                device_id={"section": lax.rem(section + away, sections), "ctx": chip},
                device_id_type=MESH,
            )

    pl.semaphore_wait(barrier, 2 * len(sides) + (peers - 1) + met)

    parts = [(0, h) + p for h in range(2) for p in plan[0]] + [(1, None) + p for p in plan[1]]

    def block(index, begin, size):
        a, h = parts[index][:2]
        return full_a.at[h, pl.ds(begin, size)] if a == 0 else relay_b.at[pl.ds(begin, size)]

    def copy(source, index, way):
        a, _, _, at, size = parts[index]
        i, sign = way
        target = block(
            index, pl.multiple_of(source * (depth_a, depth_b)[a] + at, TILE), size
        )
        return pltpu.make_async_remote_copy(
            src_ref=target,
            dst_ref=target,
            send_sem=send_sem.at[source, index],
            recv_sem=recv_sem.at[source, index],
            device_id={"ctx": me + sign * strides[i]},
            device_id_type=MESH,
        )

    def sent(source, index, times):
        target = block(index, 0, times * parts[index][4])
        return pltpu.make_async_remote_copy(
            src_ref=target,
            dst_ref=target,
            send_sem=send_sem.at[source, index],
            recv_sem=recv_sem.at[source, index],
            device_id={"ctx": partner},
            device_id_type=MESH,
        )

    def deliver(source, index):
        _, _, _, at, size = parts[index]
        span = pl.ds(pl.multiple_of(source * depth_b + at, TILE), size)
        return pltpu.make_async_remote_copy(
            src_ref=relay_b.at[span],
            dst_ref=full_b.at[span],
            send_sem=send_sem.at[source, index],
            recv_sem=whole_sem.at[0],
            device_id={"section": lax.rem(section + sections - 1, sections)},
            device_id_type=MESH,
        )

    def inside(i, place):
        return both(place >= 0, place < sizes[i])

    def goes(coords, index, way):
        h, order = parts[index][1:3]
        i, sign = way
        ok = both(inside(i, mine[i] + sign), (mine[i] - coords[i]) * sign >= 0)
        for later in order[order.index(i) + 1 :]:
            ok = both(ok, mine[later] == coords[later])
        if h is not None:
            if i == axis:
                ok = both(ok, jnp.logical_or(role != h, inside(i, mine[i] + 2 * sign)))
            else:
                ok = both(ok, role == h)
        return ok

    def onward(source, coords, index):
        for way in ways:
            @pl.when(goes(coords, index, way))
            def _(way=way):
                copy(source, index, way).start()

    def arrives(coords, index):
        h = parts[index][1]
        if h is None:
            return None
        gap = mine[axis] - coords[axis]
        beyond = jnp.where(gap > 0, inside(axis, mine[axis] + 1), inside(axis, mine[axis] - 1))
        ok = both(gap != 0, beyond)
        for i in range(d):
            if i != axis:
                ok = both(ok, mine[i] == coords[i])
        return jnp.logical_or(role == h, ok)

    def of(wanted):
        return [index for index in range(len(parts)) if parts[index][0] == wanted]

    def source_of(j):
        coords = coords_of(j)
        for i in range(d):
            if i == axis:
                coords[i] = place_in_line(mine[i], sizes[i], sizes[i] - 1 - coords[i])
            else:
                coords[i] = lax.rem(mine[i] + coords[i], sizes[i])
        return sum(c * s for c, s in zip(coords, strides)), coords

    def receive(wanted, least, most):
        @pl.loop(least * total, most * total)
        def _(k):
            hops, j = lax.div(k, total), lax.rem(k, total)
            source, coords = source_of(j)
            away = sum(jnp.abs(mine[i] - coords[i]) for i in range(d))

            @pl.when(away == hops)
            def _():
                for index in of(wanted):
                    def take(index=index):
                        copy(source, index, ways[0]).wait_recv()
                        onward(source, coords, index)
                        if wanted == 1:
                            deliver(source, index).start()

                    ok = arrives(coords, index)
                    if ok is None:
                        take()
                    else:
                        pl.when(ok)(take)

    def drain(wanted):
        @pl.loop(0, total)
        def _(source):
            coords = coords_of(source)
            for index in of(wanted):
                times = sum(goes(coords, index, way).astype(jnp.int32) for way in ways)
                ok = arrives(coords, index)
                if ok is not None:
                    times = jnp.where(jnp.logical_or(source == me, ok), times, 0)
                if wanted == 1:
                    times = times + (source != me).astype(jnp.int32)
                for n in range(1, most_ways + 1 + wanted):
                    @pl.when(times == n)
                    def _(index=index, n=n):
                        sent(source, index, n).wait_send()

    farthest = sum(n - 1 for n in sizes) + 1

    def columns(c):
        return pl.ds(pl.multiple_of(c * stripe, stripe), stripe)

    def send_x(c):
        return pltpu.make_async_remote_copy(
            src_ref=xbuf.at[role, :, :, columns(c)],
            dst_ref=xbuf.at[role, :, :, columns(c)],
            send_sem=x_send.at[2, c],
            recv_sem=x_recv.at[1, c],
            device_id={"ctx": partner},
            device_id_type=MESH,
        )

    def pass_on(to, c):
        return pltpu.make_async_remote_copy(
            src_ref=result.at[:, :, columns(c)],
            dst_ref=xbuf.at[role, :, :, columns(c)],
            send_sem=x_send.at[to, c],
            recv_sem=x_recv.at[to, c],
            device_id={"section": lax.rem(section + 1, sections), "ctx": (me, partner)[to]},
            device_id_type=MESH,
        )

    def wait_x(which, c):
        place = role if which == 0 else 1 - role
        pltpu.make_async_remote_copy(
            src_ref=result.at[:, :, columns(c)],
            dst_ref=xbuf.at[place, :, :, columns(c)],
            send_sem=x_send.at[which, c],
            recv_sem=x_recv.at[which, c],
            device_id={"ctx": partner},
            device_id_type=MESH,
        ).wait_recv()

    def put(c):
        return pltpu.make_async_copy(
            result.at[:, :, columns(c)], out.at[:, :, columns(c)], put_sem.at[c]
        )

    hand = pltpu.make_async_remote_copy(
        src_ref=shard_b,
        dst_ref=relay_b.at[pl.ds(pl.multiple_of(me * depth_b, TILE), depth_b)],
        send_sem=hand_sem.at[0],
        recv_sem=hand_sem.at[1],
        device_id={"section": lax.rem(section + 1, sections)},
        device_id_type=MESH,
    )
    send_decay = pltpu.make_async_remote_copy(
        src_ref=decay,
        dst_ref=decays,
        send_sem=d_sem.at[0],
        recv_sem=d_sem.at[1],
        device_id={"ctx": partner},
        device_id_type=MESH,
    )
    send_decay.start()
    hand.start()
    for c in staged_a:
        c.wait()

    @pl.when(section == 0)
    def _():
        for index in of(0):
            onward(me, mine, index)
        x_own.wait()

    staged_b.wait()

    at_row = lax.broadcasted_iota(jnp.int32, (rows, rows), 0)
    at_col = lax.broadcasted_iota(jnp.int32, (rows, rows), 1)
    causal = at_row >= at_col
    upper = (at_row <= at_col).astype(f32)

    def accumulate(place, source):
        spread = (
            lax.broadcasted_iota(jnp.int32, (half_heads, half_heads * lanes), 0)
            == lax.broadcasted_iota(jnp.int32, (half_heads, half_heads * lanes), 1) // lanes
        ).astype(f32)
        for m in range(micro):
            own = source[m, pl.ds(pl.multiple_of(role * half_heads, half_heads), half_heads), :]
            summed = dot(own, upper, precision=lax.Precision.HIGHEST)
            cumt[place * micro + m] = summed
            cumx[place * micro + m] = dot(
                summed, spread, ((0,), (0,)), precision=lax.Precision.HIGHEST
            )

    accumulate(role, decay)
    send_decay.wait_recv()
    accumulate(1 - role, decays)

    def let_next_start():
        pl.semaphore_signal(
            start_sem, inc=1, device_id={"section": lax.rem(section + 1, sections)},
            device_id_type=MESH,
        )

    def measure_rows(place, m):
        @pl.loop(0, rows // TILE, unroll=4)
        def _(q):
            at = pl.multiple_of(q * TILE, TILE)
            wide_rows = xbuf[place, m, pl.ds(at, TILE), :].astype(f32)
            scale = lax.rsqrt(jnp.mean(wide_rows * wide_rows, axis=-1, keepdims=True) + 1e-05)
            scales[place * micro + m, pl.ds(at, TILE), :] = jnp.broadcast_to(scale, (TILE, lanes))

    def relay_own():
        hand.wait_recv()
        for index in of(1):
            onward(me, mine, index)

    def send_stripes(least, most):
        @pl.when(section == 0)
        def _():
            for c in range(least, most):
                send_x(c).start()

    @pl.when(section > 0)
    def _():
        pl.semaphore_wait(start_sem, 1)
        relay_own()
        receive(1, 1, 3)
        for index in of(0):
            onward(me, mine, index)
        receive(1, 3, 4)
        receive(0, 1, 2)
        receive(1, 4, 5)
        receive(0, 2, 3)
        let_next_start()
        receive(1, 5, farthest)
        receive(0, 3, farthest - 1)
        for c in range(stripes):
            wait_x(0, c)
        for m in range(micro):
            measure_rows(role, m)
        for c in range(stripes):
            wait_x(1, c)
        for m in range(micro):
            measure_rows(1 - role, m)
        receive(0, farthest - 1, farthest)

    @pl.when(section == 0)
    def _():
        receive(0, 1, 2)
        send_stripes(stripes * 0 // 4, stripes * 2 // 4)
        receive(0, 2, 3)
        send_stripes(stripes * 2 // 4, stripes * 3 // 4)
        receive(0, 3, 4)
        send_stripes(stripes * 3 // 4, stripes * 4 // 4)
        let_next_start()
        for m in range(micro):
            measure_rows(role, m)
        receive(0, 4, farthest - 1)
        for c in range(stripes):
            wait_x(1, c)
        for m in range(micro):
            measure_rows(1 - role, m)
        receive(0, farthest - 1, farthest)

    def project(place):
        @pl.loop(0, 3 * half_inner // 512)
        def _(c):
            cols = pl.ds(pl.multiple_of(c * 512, 512), 512)
            inputs = xbuf[place].reshape(micro * rows, width)
            product = dot(inputs, full_a[role, :, cols])
            scale = jnp.concatenate(
                [scales[place * micro + m] for m in range(micro)], axis=0
            )
            scale = jnp.concatenate([scale] * (512 // lanes), axis=1)
            proj[place, :, cols] = (product * scale).astype(bf16)

    project(role)
    project(1 - role)

    first_half = lax.broadcasted_iota(jnp.int32, (rows, lanes), 1) < head_dim
    first_item = lax.broadcasted_iota(jnp.int32, (head_dim, lanes), 1) < head_dim
    per_pair = head_dim // part

    def located(u):
        g, p = lax.div(u, pairs), lax.rem(u, pairs)
        place, m = lax.div(g, micro), lax.rem(g, micro)
        span = pl.ds(pl.multiple_of(m * rows, TILE), rows)

        def column(which):
            return pl.ds(pl.multiple_of(which * half_inner + p * lanes, lanes), lanes)

        def cum(h):
            return cumx[g, :, pl.ds(pl.multiple_of((2 * p + h) * lanes, lanes), lanes)]

        return place, m, p, span, column, cum

    @pl.loop(0, 2 * micro * pairs, unroll=4)
    def _(u):
        place, m, p, span, column, cum = located(u)
        decayed = jnp.where(first_half, cum(0), cum(1))
        ending = decayed[rows - 1 :, :]
        scaled = (proj[place, span, column(1)].astype(f32) * jnp.exp(ending - decayed)).astype(bf16)
        state = dot(scaled, proj[place, span, column(2)], ((0,), (0,)))
        packed = jnp.where(first_item, state[:head_dim], state[head_dim:]).astype(bf16)
        weight = jnp.broadcast_to(jnp.exp(ending), (TILE, lanes)).astype(bf16)
        for piece in range(per_pair):
            to = (m * pairs + p) * per_pair + piece
            items[to, place, :part, :] = packed[piece * part : (piece + 1) * part]
            items[to, place, part:, :] = weight

    def first(to, slot_from):
        return pltpu.make_async_remote_copy(
            src_ref=items.at[to],
            dst_ref=got.at[slot_from],
            send_sem=s1.at[to],
            recv_sem=r1.at[slot_from],
            device_id={"ctx": device_of(to, role)},
            device_id_type=MESH,
        )

    def second(to, slot_from):
        return pltpu.make_async_remote_copy(
            src_ref=carried.at[to],
            dst_ref=landed.at[slot_from],
            send_sem=s2.at[to],
            recv_sem=r2.at[slot_from],
            device_id={"ctx": device_of(to, role)},
            device_id_type=MESH,
        )

    @pl.loop(1, peers)
    def _(k):
        first(lax.rem(my_peer + k, peers), my_peer).start()

    got[my_peer] = items[my_peer]

    def within(u):
        place, m, p, span, column, cum = located(u)
        queries, keys, values = (proj[place, span, column(i)] for i in range(3))
        outs = []
        for h in range(2):
            own_half = first_half if h == 0 else jnp.logical_not(first_half)
            scores = dot(jnp.where(own_half, queries, jnp.zeros_like(queries)), keys, ((1,), (1,)))
            gap = cum(h) - cumt[place * micro + m, pl.ds(2 * p + h, 1), :]
            weights = jnp.where(
                causal, scores * jnp.exp(jnp.where(causal, gap, 0.0)), 0.0
            ).astype(bf16)
            outs.append(dot(weights, values))
        intra[place, span, column(0)] = jnp.where(first_half, outs[0], outs[1])

    @pl.loop(0, micro * pairs, unroll=4)
    def _(u):
        within((1 - role) * (micro * pairs) + u)

    def step(b, acc):
        peer = peer_of(b)
        side = lax.rem(lax.rem(lax.div(b, strides[axis]), sizes[axis]), 2)

        @pl.when(both(peer != my_peer, side == 0))
        def _():
            first(peer, peer).wait_recv()

        low = acc.astype(bf16)
        carried[peer, side] = low

        @pl.when(both(peer != my_peer, side == 1))
        def _():
            second(peer, my_peer).start()

        @pl.when(peer == my_peer)
        def _():
            landed[my_peer, side] = low

        item = got[peer, side].astype(f32)
        return acc * item[part : part + 1] + item[:part]

    @pl.when(section > 0)
    def _():
        drain(0)

    lax.fori_loop(0, total, step, jnp.zeros((part, lanes), f32))

    @pl.loop(0, micro * pairs, unroll=4)
    def _(u):
        within(role * (micro * pairs) + u)

    @pl.when(section > 0)
    def _():
        drain(1)

    @pl.loop(1, peers)
    def _(k):
        peer = lax.rem(my_peer + k, peers)
        second(peer, peer).wait_recv()

    def mix(u):
        place, m, p, span, column, cum = located(u)
        low = jnp.concatenate(
            [landed[(m * pairs + p) * per_pair + i, place] for i in range(per_pair)], axis=0
        )
        none = jnp.zeros_like(low)
        block = jnp.concatenate(
            [jnp.where(first_item, low, none), jnp.where(first_item, none, low)], axis=0
        )
        decayed = jnp.where(first_half, cum(0), cum(1))
        mixture = (
            intra[place, span, column(0)]
            + dot(proj[place, span, column(0)], block) * jnp.exp(decayed)
        )
        squares = mixture * mixture
        factors = [
            lax.rsqrt(
                jnp.sum(jnp.where(own, squares, 0.0), axis=-1, keepdims=True) / head_dim + 1e-05
            )
            for own in (first_half, jnp.logical_not(first_half))
        ]
        mixed[place, span, column(0)] = (
            mixture * jnp.where(first_half, factors[0], factors[1])
        ).astype(bf16)

    send_mixed = pltpu.make_async_remote_copy(
        src_ref=mixed.at[1 - role],
        dst_ref=mixed_in,
        send_sem=mix_sem.at[0],
        recv_sem=mix_sem.at[1],
        device_id={"ctx": partner},
        device_id_type=MESH,
    )

    @pl.loop(0, micro * pairs, unroll=4)
    def _(u):
        mix((1 - role) * (micro * pairs) + u)

    send_mixed.start()

    @pl.loop(0, micro * pairs, unroll=4)
    def _(u):
        mix(role * (micro * pairs) + u)

    send_mixed.wait_recv()

    pltpu.make_async_remote_copy(
        src_ref=full_b.at[pl.ds(0, (total - 1) * depth_b)],
        dst_ref=full_b.at[pl.ds(0, (total - 1) * depth_b)],
        send_sem=hand_sem.at[0],
        recv_sem=whole_sem.at[0],
        device_id={"section": lax.rem(section + sections - 1, sections)},
        device_id_type=MESH,
    ).wait_recv()

    here = pl.ds(pl.multiple_of(role * half_inner, TILE), half_inner)
    there = pl.ds(pl.multiple_of((1 - role) * half_inner, TILE), half_inner)

    @pl.loop(0, stripes)
    def _(c):
        cols = columns(c)
        product = dot(mixed[role], full_b[here, cols]) + dot(mixed_in[...], full_b[there, cols])
        for m in range(micro):
            result[m, :, cols] = (
                xbuf[role, m, :, cols].astype(f32) + product[m * rows : (m + 1) * rows]
            ).astype(bf16)

        put(c).start()

        @pl.when(section < sections - 1)
        def _():
            for to in (1, 0):
                pass_on(to, c).start()

    @pl.when(section == 0)
    def _():
        pl.semaphore_wait(start_sem, 1)
        relay_own()
        receive(1, 1, farthest)
        drain(0)
        drain(1)
        for c in range(stripes):
            send_x(c).wait_send()

    hand.wait_send()
    send_decay.wait_send()
    send_mixed.wait_send()

    @pl.loop(1, peers)
    def _(k):
        peer = lax.rem(my_peer + k, peers)
        first(peer, my_peer).wait_send()
        second(peer, my_peer).wait_send()

    for c in range(stripes):
        put(c).wait()

    @pl.when(section < sections - 1)
    def _():
        for c in range(stripes):
            for to in range(2):
                pass_on(to, c).wait_send()


def shards(sizes, sections, tokens, qkv_weight, out_weight, log_decay):
    micro, rows, width = tokens.shape
    total = int(np.prod(sizes))
    peers = total // 2
    heads = log_decay.shape[3]
    own = (qkv_weight[0], out_weight[0])
    inner = own[1].shape[0] * total
    half = inner // 2
    lanes = 2 * inner // heads
    part = micro * inner // 2 // total
    plan = [pieces(s.shape[0], sizes, n) for s, n in zip(own, (2, 4))]
    count = 2 * len(plan[0]) + len(plan[1])
    stripes = max(1, width // 512)
    f32, bf16 = jnp.float32, jnp.bfloat16
    dma = pltpu.SemaphoreType.DMA
    anywhere = pl.BlockSpec(memory_space=pl.ANY)
    vmem = pl.BlockSpec(memory_space=pltpu.VMEM)
    result = pl.pallas_call(
        functools.partial(whole_kernel, sizes, sections, plan, heads),
        out_shape=jax.ShapeDtypeStruct(tokens.shape, tokens.dtype),
        in_specs=[anywhere, vmem, anywhere, anywhere],
        out_specs=anywhere,
        scratch_shapes=[
            pltpu.VMEM((2, width, 3 * half), bf16),
            pltpu.VMEM((inner, width), bf16),
            pltpu.VMEM((inner, width), bf16),
            pltpu.VMEM((2, micro, rows, width), bf16),
            pltpu.VMEM((2 * micro, rows, lanes), f32),
            pltpu.VMEM((2, micro * rows, 3 * half), bf16),
            pltpu.VMEM((micro, heads, rows), f32),
            pltpu.VMEM((2 * micro, rows, heads // 2 * lanes), f32),
            pltpu.VMEM((2 * micro, heads // 2, rows), f32),
            pltpu.VMEM((2, micro * rows, half), f32),
            pltpu.VMEM((2, micro * rows, half), bf16),
            pltpu.VMEM((micro * rows, half), bf16),
            pltpu.VMEM((micro, rows, width), bf16),
            pltpu.VMEM((peers, 2, part + TILE, lanes), bf16),
            pltpu.VMEM((peers, 2, part + TILE, lanes), bf16),
            pltpu.VMEM((peers, 2, part, lanes), bf16),
            pltpu.VMEM((peers, 2, part, lanes), bf16),
            dma((total, count)),
            dma((total, count)),
            dma((8,)),
            dma((3, stripes)),
            dma((2, stripes)),
            dma((stripes,)),
            dma((2,)),
            dma((2,)),
            dma((2,)),
            dma((1,)),
            pltpu.SemaphoreType.REGULAR,
            dma((peers,)),
            dma((peers,)),
            dma((peers,)),
            dma((peers,)),
        ],
        compiler_params=pltpu.CompilerParams(
            collective_id=0, has_side_effects=True, vmem_limit_bytes=60 * 2**20
        ),
        name="mixer_stack",
    )(tokens, jnp.swapaxes(log_decay[0], 1, 2), *own)
    return result[None]


def solution(mesh):
    in_specs = (
        P(None, "ctx", None),
        P("section", "ctx", None),
        P("section", "ctx", None),
        P("section", None, "ctx", None),
    )
    out_specs = P("section", None, "ctx", None)
    return jax.shard_map(
        functools.partial(shards, line_sizes(mesh), mesh.shape["section"]),
        mesh=mesh,
        in_specs=in_specs,
        out_specs=out_specs,
        check_vma=False,
    )
```
